256 devices in a mesh: grp: 4 (over y), sub: 64 (over z, x, core).
Axes of the slice: x: 4, y: 4, z: 8, core: 2. Of those that a mesh axis runs over, the one named last changes fastest.
Arguments:
- neumann: bfloat16 [4, 64, 1024, 1024], P('grp', 'sub'), may hold values from -1 to 4
- dirichlet: bfloat16 [4, 64, 1024, 1024], P('grp', 'sub'), may hold values from -1 to 4
- coarse_inverse: float32 [4, 64, 128, 2048], P('grp', 'sub'), may hold values from -1 to 3
- loads: bfloat16 [4, 64, 1024, 256], P('grp', 'sub'), may hold values from -72 to 72
- iface_sizes: int32 [4, 64], P('grp', 'sub'), may hold values from 1 to 512, 16384 in all within a row
- wave_dirs: int32 [4, 64, 32], P('grp', 'sub'), may hold values from 0 to 63
Outputs:
- dual: float32 [4, 64, 512, 256], P('grp', 'sub')
- residual: float32 [4, 64, 512, 256], P('grp', 'sub')
The draws below stay inside these ranges and needn't reach their ends.
Inputs may be any that keep to these rules, and one draw needn't show every extreme that they name: `iface_sizes`: the 64 sizes of one group sum to 16384, and in each group one size is exactly 512.
All inputs are finite; a program needn't handle non-finite values.
Results may differ from the reference program's by a relative error of at most 0.005.
Values may be sent and summed in bfloat16 or wider, within the bound.
No kernel may reach another device: no remote copies, remote signals or barrier semaphores. Data moves between devices by JAX's collectives and lax.ppermute only.
A program may use at most 64 MiB of HBM per device.

```python
import math
import jax
import jax.numpy as jnp
import numpy as np
from jax import lax

NB = 1024
WAVES = 32
NDIR = 64
RHS = 256
ITERS = 2
KMAX = 512
N_GRP = 4
N_SUB = 64


def schur_draw(key, low, high):
    keys = jax.random.split(key, N_GRP * N_SUB)

    def single(one_key):
        noise_key, diag_key = jax.random.split(one_key)
        noise = jnp.clip(jax.random.normal(noise_key, (NB, NB), jnp.float32), -5.0, 5.0)
        symmetric = (noise + noise.T) * (0.6 / jnp.sqrt(2.0 * NB))
        diagonal = jax.random.uniform(diag_key, (NB,), jnp.float32, low, high)
        return (symmetric + jnp.diag(diagonal)).astype(jnp.bfloat16)
    return lax.map(single, keys).reshape(N_GRP, N_SUB, NB, NB)


def draw_neumann(key, part):
    return schur_draw(jax.random.fold_in(key, 11), 1.5, 3.0)


def draw_dirichlet(key, part):
    return schur_draw(jax.random.fold_in(key, 23), 1.5, 3.0)


def draw_coarse_inverse(key, part):
    total_rows = N_GRP * WAVES
    total_cols = N_SUB * WAVES
    count = N_GRP * N_SUB
    keys = jax.random.split(jax.random.fold_in(key, 37), count)
    factor = 0.8 / jnp.sqrt(1.0 * N_GRP * N_SUB * WAVES)

    def single(pair):
        index, one_key = pair
        noise_key, diag_key = jax.random.split(one_key)
        noise = jnp.clip(jax.random.normal(noise_key, (total_rows, total_cols), jnp.float32), -5.0, 5.0)
        group = index // N_SUB
        member = index % N_SUB
        row_ids = jnp.arange(total_rows)[:, None]
        col_ids = jnp.arange(total_cols)[None, :]
        on_diag = (row_ids // WAVES == group) & (col_ids // WAVES == member) & (row_ids % WAVES == col_ids % WAVES)
        diagonal = jax.random.uniform(diag_key, (total_rows, total_cols), jnp.float32, 1.0, 2.0)
        return noise * factor + jnp.where(on_diag, diagonal, 0.0)
    tiles = lax.map(single, (jnp.arange(count), keys))
    return tiles.reshape(N_GRP, N_SUB, total_rows, total_cols)


def draw_loads(key, part):
    keys = jax.random.split(jax.random.fold_in(key, 53), 3)
    shape = (N_GRP, N_SUB, NB, RHS)
    place = jnp.arange(N_GRP * N_SUB).astype(jnp.float32).reshape(N_GRP, N_SUB, 1, 1) / (N_GRP * N_SUB - 1)
    noise = jnp.clip(jax.random.normal(keys[0], shape, jnp.float32), -4.0, 4.0)
    ramp = 1.0 + place
    row_scale = jnp.exp(jax.random.uniform(keys[1], (N_GRP, N_SUB, NB, 1), jnp.float32, jnp.log(0.3), jnp.log(3.0)))
    col_scale = jnp.exp(jax.random.uniform(keys[2], (1, 1, 1, RHS), jnp.float32, jnp.log(0.5), jnp.log(2.0)))
    return (noise * row_scale * col_scale * ramp).astype(jnp.bfloat16)


def plant(result, own_key, low, top_value):
    spot = [jax.random.randint(jax.random.fold_in(own_key, axis), (), 0, length) for axis, length in enumerate(result.shape)]
    main_axis = result.shape.index(max(result.shape))
    neighbour = spot[:main_axis] + [(spot[main_axis] + 1) % result.shape[main_axis]] + spot[main_axis + 1:]
    return result.at[tuple(spot)].set(low).at[tuple(neighbour)].set(top_value)


def profile(number_of, total, most, skew):
    portions = [(1 << 20) // math.isqrt(rank ** skew) + 1 for rank in range(2, number_of + 1)]
    surplus, counts = total - most - (number_of - 1), [1] * (number_of - 1)
    while surplus > 0:
        movable = [i for i in range(number_of - 1) if counts[i] < most]
        whole, remaining = sum([portions[i] for i in movable]), surplus
        for i in movable:
            extra = min(most - counts[i], max(1, remaining * portions[i] // whole), surplus)
            counts[i] = counts[i] + extra
            surplus = surplus - extra
    return np.array([most] + counts)


def ragged(own_key, count, total, bound, skew):
    if count == 2:
        one = jax.random.randint(own_key, (), max(1, total - bound), min(bound, total - 1) + 1)
        return jnp.stack([one, total - one])
    lengths = jnp.asarray(profile(count, total, bound, skew), jnp.int32)
    couples = (count - 1) // 2
    source_of, receiver = lengths[1:1 + 2 * couples:2], lengths[2:2 + 2 * couples:2]
    slack = jnp.minimum(source_of - 1, bound - receiver)
    shifted = jax.random.randint(jax.random.fold_in(own_key, 1), (couples,), 0, 1 << 20) % (slack + 1)
    lengths = lengths.at[1:1 + 2 * couples:2].set(source_of - shifted).at[2:2 + 2 * couples:2].set(receiver + shifted)
    return lengths[jax.random.permutation(jax.random.fold_in(own_key, 2), count)]


def setup_inputs(seed: int = 0) -> dict:
    seeds = jax.random.split(jax.random.key(seed), 7)
    return {
        "neumann": draw_neumann(jax.random.fold_in(seeds[6], 71), 0),
        "dirichlet": draw_dirichlet(jax.random.fold_in(seeds[6], 71), 0),
        "coarse_inverse": draw_coarse_inverse(jax.random.fold_in(seeds[6], 71), 0),
        "loads": draw_loads(jax.random.fold_in(seeds[6], 71), 0),
        "iface_sizes": jax.vmap(lambda own: ragged(own, N_SUB, N_SUB * KMAX // 2, KMAX, 2))(jax.random.split(seeds[4], N_GRP)).reshape((N_GRP, N_SUB)).astype(jnp.int32),
        "wave_dirs": plant(jax.random.randint(seeds[5], (N_GRP, N_SUB, WAVES), 0, NDIR), jax.random.fold_in(seeds[5], 1), 0, NDIR - 1).astype(jnp.int32),
    }


wave_number = 0.785
highest = lax.Precision.HIGHEST

def make_waves(iface_sizes, wave_dirs):
    rows = jnp.arange(KMAX).astype(jnp.float32)
    live = (jnp.arange(KMAX)[None, None, :] < iface_sizes[:, :, None]).astype(jnp.float32)
    angle = 2.0 * jnp.pi * wave_dirs.astype(jnp.float32) / NDIR
    phase = (jnp.arange(WAVES) % 2).astype(jnp.float32) * (jnp.pi / 2.0)
    basis = jnp.cos(wave_number * rows[None, None, :, None] * jnp.cos(angle)[:, :, None, :] + phase)
    return (basis * live[..., None] / jnp.sqrt(jnp.float32(KMAX)), live)

def spread(values):
    left = jnp.roll(values, 1, axis=1)
    middle = jnp.zeros((N_GRP, N_SUB, NB - 2 * KMAX, RHS), jnp.bfloat16)
    return jnp.concatenate([-left, middle, jnp.flip(values, 2)], axis=2)

def product_ends(mats, vectors):

    def single(pair):
        product = jnp.dot(pair[0], pair[1], preferred_element_type=jnp.float32)
        return (product[:KMAX], product[NB - KMAX:])
    heads, tails = lax.map(single, (mats.reshape(-1, NB, NB), vectors.reshape(-1, NB, RHS)))
    return (heads.reshape(N_GRP, N_SUB, KMAX, RHS), tails.reshape(N_GRP, N_SUB, KMAX, RHS))

def jump(heads, tails, live):
    return (jnp.flip(tails, 2) - jnp.roll(heads, -1, axis=1)) * live[..., None]

def apply_op(mats, values, live):
    heads, tails = product_ends(mats, spread(values.astype(jnp.bfloat16)))
    return jump(heads, tails, live)

def correct(values, basis, tiles):
    coef = jnp.einsum('gskm,gskr->gsmr', basis, values, precision=highest)
    whole = coef.reshape(N_GRP, N_SUB * WAVES, RHS)
    terms = jnp.einsum('gsac,gcr->gsar', tiles, whole, precision=highest)
    summed = terms.reshape(N_GRP, N_SUB, N_GRP, WAVES, RHS).sum(axis=0)
    summed = jnp.transpose(summed, (1, 0, 2, 3))
    return jnp.einsum('gskm,gsmr->gskr', basis, summed, precision=highest)

def reference(neumann, dirichlet, coarse_inverse, loads, iface_sizes, wave_dirs):
    basis, live = make_waves(iface_sizes, wave_dirs)
    heads, tails = product_ends(neumann, loads)
    dual_rhs = jump(heads, tails, live)
    dual = correct(dual_rhs, basis, coarse_inverse)
    residual = dual_rhs - apply_op(neumann, dual, live)
    direction = dual_rhs
    rho_prev = jnp.ones((RHS,), jnp.float32)
    for step in range(ITERS):
        projected = residual - correct(residual, basis, coarse_inverse)
        precond = apply_op(dirichlet, projected, live)
        rho = lax.optimization_barrier(jnp.sum(projected * precond, axis=(0, 1, 2)))
        search = precond - correct(precond, basis, coarse_inverse)
        if step == 0:
            direction = search
        else:
            direction = search + rho / rho_prev * direction
        image = apply_op(neumann, direction, live)
        alpha = rho / lax.optimization_barrier(jnp.sum(direction * image, axis=(0, 1, 2)))
        dual = dual + alpha * direction
        residual = residual - alpha * image
        rho_prev = rho
    return (dual, residual)
```

```python
import functools

import jax
import jax.numpy as jnp
from jax import lax
from jax.experimental import pallas as pl
from jax.experimental.pallas import tpu as pltpu
from jax.sharding import Mesh
from jax.sharding import PartitionSpec as P

NDIR = 64
ITERS = 2
WAVE_NUMBER = 0.785
SUB = ("z", "x", "c")
SPREAD = ("grp", "x", "c")
F32 = jnp.float32
BF16 = jnp.bfloat16


def call(body, outs, name, flops=0, size=0):
    return pl.pallas_call(
        body,
        out_shape=[jax.ShapeDtypeStruct(shape, dtype) for shape, dtype in outs],
        name=name,
        cost_estimate=pl.CostEstimate(flops=flops, bytes_accessed=size, transcendentals=0),
    )


def mm(a, b):
    return jnp.dot(a, b, preferred_element_type=F32)


def halves(value):
    high = value.astype(BF16)
    return high, (value - high.astype(F32)).astype(BF16)


def mm_wide(pair, value):
    high, low = halves(value)
    return mm(pair[0], high) + (mm(pair[0], low) + mm(pair[1], high))


def reversal(n):
    rows = lax.broadcasted_iota(jnp.int32, (n, n), 0)
    cols = lax.broadcasted_iota(jnp.int32, (n, n), 1)
    return (rows + cols == n - 1).astype(BF16)


def live_rows(size_ref, shape):
    return lax.broadcasted_iota(jnp.int32, shape, 0) < size_ref[0, 0]


def wave_parts(size, directions, reach):
    def basis(axis):
        def along(v):
            return v[:, None] if axis == 0 else v[None, :]

        def across(v):
            return v[None, :] if axis == 0 else v[:, None]

        rows = jnp.arange(reach).astype(F32)
        live = (jnp.arange(reach) < size).astype(F32)
        angle = 2.0 * jnp.pi * directions.astype(F32) / NDIR
        phase = (jnp.arange(directions.shape[0]) % 2).astype(F32) * (jnp.pi / 2.0)
        wave = jnp.cos(WAVE_NUMBER * along(rows) * across(jnp.cos(angle)) + across(phase))
        wave = wave * along(live) / jnp.sqrt(F32(reach))
        high = lax.reduce_precision(wave, 8, 7)
        return high.astype(BF16), (wave - high).astype(BF16)

    return basis(0), basis(1)


def pack(rows, extra, out_ref, copies, reach):
    waves, columns = rows.shape
    half = columns // 2
    for i in copies:
        out_ref[i, 0:waves] = rows[:, :half]
        out_ref[i, waves : 2 * waves] = rows[:, half:]
        if extra is not None:
            out_ref[i, 2 * waves : 2 * waves + 1] = extra[:, :half]
            out_ref[i, 2 * waves + 1 : 2 * waves + 2] = extra[:, half:]


def unpack(value, waves, extra):
    rows = jnp.concatenate([value[0:waves], value[waves : 2 * waves]], axis=1)
    if not extra:
        return rows, None
    last = jnp.concatenate(
        [value[2 * waves : 2 * waves + 1], value[2 * waves + 1 : 2 * waves + 2]], axis=1
    )
    return rows, last


def heads_kernel(mat_ref, loads_ref, out_ref):
    reach = out_ref.shape[0]
    out_ref[...] = mm(mat_ref[0:reach], loads_ref[...])


def turn_kernel(mat_ref, own_ref, away_ref):
    reach = own_ref.shape[0]
    flip = reversal(reach)
    low = mm(flip, mat_ref[reach:]).astype(BF16)
    own_ref[:, 0:reach] = mm(low[:, reach:], flip).astype(BF16)
    own_ref[:, reach:] = low[:, :reach]
    away_ref[:, 0:reach] = mat_ref[0:reach, 0:reach]
    away_ref[:, reach:] = mm(mat_ref[0:reach, reach:], flip).astype(BF16)


def tile_kernel(near, far, tile_ref, out_ref):
    rows, total = tile_ref.shape
    waves = total // (near * far)
    high, low = halves(tile_ref[...])
    for part, value in enumerate((high, low)):
        for j in range(near):
            pieces = [
                value[:, (k * near + j) * waves : (k * near + j + 1) * waves] for k in range(far)
            ]
            out_ref[j, part * rows : (part + 1) * rows] = jnp.concatenate(pieces, axis=1)


def rhs_kernel(size_ref, mat_ref, loads_ref, heads_ref, wt_hi, wt_lo, rhs_ref, pay_ref):
    reach = rhs_ref.shape[0]
    low = mm(mat_ref[reach:], loads_ref[...])
    flip = reversal(reach)
    high_part = low.astype(BF16)
    rest = low - high_part.astype(F32)
    mid_part = rest.astype(BF16)
    low_part = (rest - mid_part.astype(F32)).astype(BF16)
    tails = mm(flip, high_part) + (mm(flip, mid_part) + mm(flip, low_part))
    rhs = jnp.where(live_rows(size_ref, tails.shape), tails - heads_ref[...], 0.0)
    rhs_ref[...] = rhs
    rows = mm_wide((wt_hi[...], wt_lo[...]), rhs)
    pack(rows, None, pay_ref, range(pay_ref.shape[0]), reach)


def apply_kernel(mode, size_ref, own_ref, away_ref, x_ref, xr_ref, prev_ref, next_ref, wt_hi, wt_lo, *rest):
    xr = xr_ref[...]
    product = mm(own_ref[...], jnp.concatenate([xr, -prev_ref[...]], axis=0)) + mm(
        away_ref[...], jnp.concatenate([xr, -next_ref[...]], axis=0)
    )
    product = jnp.where(live_rows(size_ref, product.shape), product, 0.0)
    if mode == "start":
        rhs_ref, out_ref, pay_ref = rest
        product = rhs_ref[...] - product
        extra = None
    else:
        out_ref, pay_ref = rest
        extra = jnp.sum(x_ref[...] * product, axis=0, keepdims=True)
    out_ref[...] = product
    if mode == "last":
        half = extra.shape[1] // 2
        for i in range(pay_ref.shape[0]):
            pay_ref[i, 0:1] = extra[:, :half]
            pay_ref[i, 1:2] = extra[:, half:]
        return
    rows = mm_wide((wt_hi[...], wt_lo[...]), product)
    pack(rows, extra, pay_ref, range(pay_ref.shape[0]), 0)


def coarse_kernel(extra, groups, tiles_ref, got_ref, out_ref):
    near, twice, depth = tiles_ref.shape
    height = twice // 2
    waves = height // groups
    far = got_ref.shape[0]
    parts = [unpack(got_ref[k], waves, extra) for k in range(far)]
    stacked = jnp.concatenate([p[0] for p in parts], axis=0)
    row = sum([p[1] for p in parts[1:]], parts[0][1]) if extra else None
    high, low = halves(stacked)
    for j in range(near):
        top = tiles_ref[j, 0:height]
        value = mm(top, high) + (mm(top, low) + mm(tiles_ref[j, height:], high))
        for h in range(groups):
            pack(value[h * waves : (h + 1) * waves], row, out_ref, (h * near + j,), 0)


def summed(ref):
    total = ref[0]
    for i in range(1, ref.shape[0]):
        total = total + ref[i]
    return total


def lift(w_hi, w_lo, rows):
    return mm_wide((w_hi[...], w_lo[...]), rows)


def first_kernel(got_ref, w_hi, w_lo, dual_ref, dualr_ref):
    rows, _ = unpack(summed(got_ref), w_hi.shape[1], False)
    dual = lift(w_hi, w_lo, rows)
    dual_ref[...] = dual
    dualr_ref[...] = dual.astype(BF16)


def project_kernel(got_ref, w_hi, w_lo, res_ref, rows_ref, out_ref, outr_ref):
    rows, _ = unpack(summed(got_ref), w_hi.shape[1], False)
    rows_ref[...] = rows
    out = res_ref[...] - lift(w_hi, w_lo, rows)
    out_ref[...] = out
    outr_ref[...] = out.astype(BF16)


def search_kernel(first, got_ref, w_hi, w_lo, pre_ref, *rest):
    rows, rho = unpack(summed(got_ref), w_hi.shape[1], True)
    out = pre_ref[...] - lift(w_hi, w_lo, rows)
    if first:
        rho_ref, out_ref, outr_ref = rest
    else:
        old_rho, old_dir, rho_ref, out_ref, outr_ref = rest
        out = out + rho / old_rho[0:1] * old_dir[...]
    rho_ref[...] = jnp.broadcast_to(rho, rho_ref.shape)
    out_ref[...] = out
    outr_ref[...] = out.astype(BF16)


def step_kernel(got_ref, w_hi, w_lo, rho_ref, dir_ref, img_ref, dual_ref, res_ref, rows_ref,
                new_dual, new_res, new_out, new_outr):
    rows, bottom = unpack(summed(got_ref), w_hi.shape[1], True)
    alpha = rho_ref[0:1] / bottom
    new_dual[...] = dual_ref[...] + alpha * dir_ref[...]
    res = res_ref[...] - alpha * img_ref[...]
    new_res[...] = res
    out = res - lift(w_hi, w_lo, rows_ref[...] - alpha * rows)
    new_out[...] = out
    new_outr[...] = out.astype(BF16)


def partial_kernel(got_ref, out_ref):
    total = summed(got_ref)
    for i in range(out_ref.shape[0]):
        out_ref[i] = total


def final_kernel(got_ref, rho_ref, dir_ref, img_ref, dual_ref, res_ref, new_dual, new_res):
    total = summed(got_ref)
    bottom = jnp.concatenate([total[0:1], total[1:2]], axis=1)
    alpha = rho_ref[0:1] / bottom
    new_dual[...] = dual_ref[...] + alpha * dir_ref[...]
    new_res[...] = res_ref[...] - alpha * img_ref[...]


def passed_along(block, distance):
    n = lax.axis_size(SUB)
    return lax.ppermute(block, SUB, [((i - distance) % n, i) for i in range(n)])


def exchange(value, axes):
    return lax.all_to_all(value, axes, 0, 0, tiled=True)


def shards(neumann, dirichlet, coarse_inverse, loads, iface_sizes, wave_dirs):
    nmat, dmat = neumann[0, 0], dirichlet[0, 0]
    tile, load = coarse_inverse[0, 0], loads[0, 0]
    width, columns = load.shape
    reach = width // 2
    directions = wave_dirs[0, 0]
    waves = directions.shape[0]
    groups = lax.axis_size("grp")
    far = lax.axis_size("z")
    near = lax.axis_size("x") * lax.axis_size("c")
    half = columns // 2
    size = iface_sizes
    field, rounded = ((reach, columns), F32), ((reach, columns), BF16)

    heads, = call(heads_kernel, [field], "heads", 2 * reach * width * columns, 2 << 20)(nmat, load)
    heads = passed_along(heads, -1)
    spread, = call(
        functools.partial(tile_kernel, near, far),
        [((near, 2 * tile.shape[0], tile.shape[1] // near), BF16)],
        "tile",
        size=2 << 20,
    )(tile)
    tiles = exchange(spread, ("x", "c"))
    turn = call(turn_kernel, [((reach, width), BF16)] * 2, "turn", 6 * reach**3, 4 << 20)
    n_own, n_away = turn(nmat)
    n_away = passed_along(n_away, -1)
    d_own, d_away = turn(dmat)
    d_away = passed_along(d_away, -1)

    (w_hi, w_lo), (wt_hi, wt_lo) = wave_parts(size[0, 0], directions, reach)

    short, tall = 2 * waves, 2 * waves + 8
    flops = 2 * reach * 2 * width * columns

    def pay(rows):
        return ((far, rows, half), F32)

    def solve(payload, extra):
        got = exchange(payload, "z")
        terms, = call(
            functools.partial(coarse_kernel, extra, groups),
            [((groups * near, got.shape[1], half), F32)],
            "coarse",
            6 * near * 4 * waves * far * waves * columns,
            2 << 20,
        )(tiles, got)
        return exchange(terms, SPREAD)

    def halo(rounded_x):
        return passed_along(rounded_x, 1), passed_along(rounded_x, -1)

    def apply(mode, mats, x, xr, rows, *rest):
        before, after = halo(xr)
        smem = pl.BlockSpec(memory_space=pltpu.SMEM)
        vmem = pl.BlockSpec(memory_space=pltpu.VMEM)
        count = 8 + len(rest)
        return pl.pallas_call(
            functools.partial(apply_kernel, mode),
            out_shape=[
                jax.ShapeDtypeStruct(*field),
                jax.ShapeDtypeStruct(*pay(rows)),
            ],
            in_specs=[smem] + [vmem] * count,
            name="apply_" + mode,
            cost_estimate=pl.CostEstimate(flops=flops, bytes_accessed=4 << 20, transcendentals=0),
        )(size, mats[0], mats[1], x, xr, before, after, wt_hi, wt_lo, *rest)

    rhs, payload = pl.pallas_call(
        rhs_kernel,
        out_shape=[jax.ShapeDtypeStruct(*field), jax.ShapeDtypeStruct(*pay(short))],
        in_specs=[pl.BlockSpec(memory_space=pltpu.SMEM)]
        + [pl.BlockSpec(memory_space=pltpu.VMEM)] * 5,
        name="rhs",
    )(size, nmat, load, heads, wt_hi, wt_lo)

    n_mats, d_mats = (n_own, n_away), (d_own, d_away)
    dual, dual_r = call(first_kernel, [field, rounded], "first")(solve(payload, False), w_hi, w_lo)
    res, payload = apply("start", n_mats, dual, dual_r, short, rhs)
    rows, x, xr = call(
        project_kernel, [((waves, columns), F32), field, rounded], "project"
    )(solve(payload, False), w_hi, w_lo, res)
    rho = direction = None
    for step in range(ITERS):
        pre, payload = apply("mid", d_mats, x, xr, tall)
        old = () if step == 0 else (rho, direction)
        rho, direction, dir_r = call(
            functools.partial(search_kernel, step == 0),
            [((8, columns), F32), field, rounded],
            "search",
        )(solve(payload, True), w_hi, w_lo, pre, *old)
        if step < ITERS - 1:
            image, payload = apply("mid", n_mats, direction, dir_r, tall)
            dual, res, x, xr = call(step_kernel, [field, field, field, rounded], "step")(
                solve(payload, True), w_hi, w_lo, rho, direction, image, dual, res, rows
            )
        else:
            image, payload = apply("last", n_mats, direction, dir_r, 8)
            got = exchange(payload, "z")
            terms, = call(partial_kernel, [((groups * near, 8, half), F32)], "partial")(got)
            dual, res = call(final_kernel, [field, field], "final")(
                exchange(terms, SPREAD), rho, direction, image, dual, res
            )
    return dual[None, None], res[None, None]


def solution(mesh):
    finer = Mesh(mesh.devices.reshape(mesh.shape["grp"], 8, 4, 2), ("grp", "z", "x", "c"))
    spec = P("grp", SUB, None, None)
    return jax.shard_map(
        shards,
        mesh=finer,
        in_specs=(spec, spec, spec, spec, P("grp", SUB), P("grp", SUB, None)),
        out_specs=(spec, spec),
        check_vma=False,
    )
```

```python
import functools

import jax
import jax.numpy as jnp
from jax import lax
from jax.experimental import pallas as pl
from jax.experimental.pallas import tpu as pltpu
from jax.sharding import Mesh
from jax.sharding import PartitionSpec as P

NDIR = 64
ITERS = 2
WAVE_NUMBER = 0.785
SUB = ("z", "x", "c")
SPREAD = ("grp", "x", "c")
F32 = jnp.float32
BF16 = jnp.bfloat16
GRANT = pltpu.CompilerParams(vmem_limit_bytes=20 << 20)


def call(body, outs, name, flops=0, size=0):
    return pl.pallas_call(
        body,
        out_shape=[jax.ShapeDtypeStruct(shape, dtype) for shape, dtype in outs],
        name=name,
        compiler_params=GRANT,
        cost_estimate=pl.CostEstimate(flops=flops, bytes_accessed=size, transcendentals=0),
    )


def mm(a, b):
    return jnp.dot(a, b, preferred_element_type=F32)


def halves(value):
    high = value.astype(BF16)
    return high, (value - high.astype(F32)).astype(BF16)


def mm_wide(pair, value):
    high, low = halves(value)
    return mm(pair[0], high) + (mm(pair[0], low) + mm(pair[1], high))


def reversal(n):
    rows = lax.broadcasted_iota(jnp.int32, (n, n), 0)
    cols = lax.broadcasted_iota(jnp.int32, (n, n), 1)
    return (rows + cols == n - 1).astype(BF16)


def live_rows(size_ref, shape):
    return lax.broadcasted_iota(jnp.int32, shape, 0) < size_ref[0, 0]


def wave_parts(size, directions, reach):
    def basis(axis):
        def along(v):
            return v[:, None] if axis == 0 else v[None, :]

        def across(v):
            return v[None, :] if axis == 0 else v[:, None]

        rows = jnp.arange(reach).astype(F32)
        live = (jnp.arange(reach) < size).astype(F32)
        angle = 2.0 * jnp.pi * directions.astype(F32) / NDIR
        phase = (jnp.arange(directions.shape[0]) % 2).astype(F32) * (jnp.pi / 2.0)
        wave = jnp.cos(WAVE_NUMBER * along(rows) * across(jnp.cos(angle)) + across(phase))
        wave = wave * along(live) / jnp.sqrt(F32(reach))
        high = lax.reduce_precision(wave, 8, 7)
        return high.astype(BF16), (wave - high).astype(BF16)

    return basis(0), basis(1)


STEPS = 14


def exponent(value):
    return jnp.ceil(jnp.log2(jnp.maximum(value, 1e-30)))


def scale_of(power):
    return jnp.exp2(STEPS - power)


def side_by_side(rows):
    half = rows.shape[1] // 2
    return [rows[:, :half], rows[:, half:]]


def coded_sum(extra):
    power = exponent(jnp.abs(extra))
    value = extra * scale_of(power)
    first = jnp.round(value)
    rest = jnp.round((value - first) * 2.0**STEPS)
    return side_by_side(power) + side_by_side(first) + side_by_side(rest)


def pack(blocks, code, out_ref, copies):
    count, waves, columns = blocks.shape
    half = columns // 2
    power = exponent(jnp.max(jnp.abs(blocks), axis=1))
    scaled = jnp.round(blocks * scale_of(power)[:, None, :]).astype(jnp.int32).astype(jnp.int16)
    for k in range(count):
        tail = side_by_side(power[k : k + 1]) + code
        tail = jnp.concatenate(tail, axis=0).astype(jnp.int32).astype(jnp.int16)
        for i in copies[k]:
            out_ref[i, 0:waves] = scaled[k, :, :half]
            out_ref[i, waves : 2 * waves] = scaled[k, :, half:]
            out_ref[i, 2 * waves :] = tail


def no_sum(columns):
    return [jnp.zeros((1, columns // 2), F32)] * 6


def wide(value):
    return value.astype(jnp.int32).astype(F32)


def unpack(value, waves, extra):
    tail = wide(value[2 * waves :])
    back = 1.0 / scale_of(tail[0:4])
    rows = jnp.concatenate(
        [wide(value[0:waves]) * back[0:1], wide(value[waves : 2 * waves]) * back[1:2]], axis=1
    )
    if not extra:
        return rows, None
    sums = (tail[4:6] + tail[6:8] * 2.0**-STEPS) * back[2:4]
    return rows, jnp.concatenate([sums[0:1], sums[1:2]], axis=1)


def heads_kernel(mat_ref, loads_ref, out_ref):
    reach = out_ref.shape[0]
    out_ref[...] = mm(mat_ref[0:reach], loads_ref[...])


def turn_kernel(mat_ref, own_ref, away_ref):
    reach = own_ref.shape[0]
    flip = reversal(reach)
    low = mm(flip, mat_ref[reach:]).astype(BF16)
    own_ref[:, 0:reach] = mm(low[:, reach:], flip).astype(BF16)
    own_ref[:, reach:] = low[:, :reach]
    away_ref[:, 0:reach] = mat_ref[0:reach, 0:reach]
    away_ref[:, reach:] = mm(mat_ref[0:reach, reach:], flip).astype(BF16)


def tile_kernel(near, far, tile_ref, out_ref):
    rows, total = tile_ref.shape
    waves = total // (near * far)
    high, low = halves(tile_ref[...])
    for part, value in enumerate((high, low)):
        for j in range(near):
            pieces = [
                value[:, (k * near + j) * waves : (k * near + j + 1) * waves] for k in range(far)
            ]
            out_ref[j, part * rows : (part + 1) * rows] = jnp.concatenate(pieces, axis=1)


def rhs_kernel(size_ref, mat_ref, loads_ref, heads_ref, wt_hi, wt_lo, rhs_ref, pay_ref):
    reach = rhs_ref.shape[0]
    low = mm(mat_ref[reach:], loads_ref[...])
    flip = reversal(reach)
    high_part = low.astype(BF16)
    rest = low - high_part.astype(F32)
    mid_part = rest.astype(BF16)
    low_part = (rest - mid_part.astype(F32)).astype(BF16)
    tails = mm(flip, high_part) + (mm(flip, mid_part) + mm(flip, low_part))
    rhs = jnp.where(live_rows(size_ref, tails.shape), tails - heads_ref[...], 0.0)
    rhs_ref[...] = rhs
    rows = mm_wide((wt_hi[...], wt_lo[...]), rhs)
    pack(rows[None], no_sum(rows.shape[1]), pay_ref, [range(pay_ref.shape[0])])


def apply_kernel(mode, size_ref, own_ref, away_ref, x_ref, xr_ref, prev_ref, next_ref, wt_hi, wt_lo, *rest):
    xr = xr_ref[...]
    product = mm(own_ref[...], jnp.concatenate([xr, -prev_ref[...]], axis=0)) + mm(
        away_ref[...], jnp.concatenate([xr, -next_ref[...]], axis=0)
    )
    product = jnp.where(live_rows(size_ref, product.shape), product, 0.0)
    if mode == "start":
        rhs_ref, out_ref, pay_ref = rest
        product = rhs_ref[...] - product
        extra = None
    else:
        out_ref, pay_ref = rest
        extra = jnp.sum(x_ref[...] * product, axis=0, keepdims=True)
    out_ref[...] = product
    if mode == "last":
        half = extra.shape[1] // 2
        for i in range(pay_ref.shape[0]):
            pay_ref[i, 0:1] = extra[:, :half]
            pay_ref[i, 1:2] = extra[:, half:]
        return
    rows = mm_wide((wt_hi[...], wt_lo[...]), product)
    code = no_sum(rows.shape[1]) if extra is None else coded_sum(extra)
    pack(rows[None], code, pay_ref, [range(pay_ref.shape[0])])


def coarse_kernel(extra, groups, tiles_ref, got_ref, out_ref):
    near, twice, depth = tiles_ref.shape
    height = twice // 2
    waves = height // groups
    far = got_ref.shape[0]
    parts = [unpack(got_ref[k], waves, extra) for k in range(far)]
    stacked = jnp.concatenate([p[0] for p in parts], axis=0)
    if extra:
        code = coded_sum(sum([p[1] for p in parts[1:]], parts[0][1]))
    else:
        code = no_sum(stacked.shape[1])
    high, low = halves(stacked)
    for j in range(near):
        top = tiles_ref[j, 0:height]
        value = mm(top, high) + (mm(top, low) + mm(tiles_ref[j, height:], high))
        blocks = value.reshape(groups, waves, value.shape[1])
        pack(blocks, code, out_ref, [(h * near + j,) for h in range(groups)])


def summed(ref):
    total = ref[0]
    for i in range(1, ref.shape[0]):
        total = total + ref[i]
    return total


def gathered(ref, waves, extra):
    rows, row = unpack(ref[0], waves, extra)
    for i in range(1, ref.shape[0]):
        more, more_row = unpack(ref[i], waves, extra)
        rows = rows + more
        row = row + more_row if extra else None
    return rows, row


def lift(w_hi, w_lo, rows):
    return mm_wide((w_hi[...], w_lo[...]), rows)


def first_kernel(got_ref, w_hi, w_lo, dual_ref, dualr_ref):
    rows, _ = gathered(got_ref, w_hi.shape[1], False)
    dual = lift(w_hi, w_lo, rows)
    dual_ref[...] = dual
    dualr_ref[...] = dual.astype(BF16)


def project_kernel(got_ref, w_hi, w_lo, res_ref, rows_ref, out_ref, outr_ref):
    rows, _ = gathered(got_ref, w_hi.shape[1], False)
    rows_ref[...] = rows
    out = res_ref[...] - lift(w_hi, w_lo, rows)
    out_ref[...] = out
    outr_ref[...] = out.astype(BF16)


def search_kernel(first, got_ref, w_hi, w_lo, pre_ref, *rest):
    rows, rho = gathered(got_ref, w_hi.shape[1], True)
    out = pre_ref[...] - lift(w_hi, w_lo, rows)
    if first:
        rho_ref, out_ref, outr_ref = rest
    else:
        old_rho, old_dir, rho_ref, out_ref, outr_ref = rest
        out = out + rho / old_rho[0:1] * old_dir[...]
    rho_ref[...] = jnp.broadcast_to(rho, rho_ref.shape)
    out_ref[...] = out
    outr_ref[...] = out.astype(BF16)


def step_kernel(got_ref, w_hi, w_lo, rho_ref, dir_ref, img_ref, dual_ref, res_ref, rows_ref,
                new_dual, new_res, new_out, new_outr):
    rows, bottom = gathered(got_ref, w_hi.shape[1], True)
    alpha = rho_ref[0:1] / bottom
    new_dual[...] = dual_ref[...] + alpha * dir_ref[...]
    res = res_ref[...] - alpha * img_ref[...]
    new_res[...] = res
    out = res - lift(w_hi, w_lo, rows_ref[...] - alpha * rows)
    new_out[...] = out
    new_outr[...] = out.astype(BF16)


def partial_kernel(got_ref, out_ref):
    total = summed(got_ref)
    for i in range(out_ref.shape[0]):
        out_ref[i] = total


def final_kernel(got_ref, rho_ref, dir_ref, img_ref, dual_ref, res_ref, new_dual, new_res):
    total = summed(got_ref)
    bottom = jnp.concatenate([total[0:1], total[1:2]], axis=1)
    alpha = rho_ref[0:1] / bottom
    new_dual[...] = dual_ref[...] + alpha * dir_ref[...]
    new_res[...] = res_ref[...] - alpha * img_ref[...]


def passed_along(block, distance):
    n = lax.axis_size(SUB)
    return lax.ppermute(block, SUB, [((i - distance) % n, i) for i in range(n)])


def exchange(value, axes):
    return lax.all_to_all(value, axes, 0, 0, tiled=True)


def shards(neumann, dirichlet, coarse_inverse, loads, iface_sizes, wave_dirs):
    nmat, dmat = neumann[0, 0], dirichlet[0, 0]
    tile, load = coarse_inverse[0, 0], loads[0, 0]
    width, columns = load.shape
    reach = width // 2
    directions = wave_dirs[0, 0]
    waves = directions.shape[0]
    groups = lax.axis_size("grp")
    far = lax.axis_size("z")
    near = lax.axis_size("x") * lax.axis_size("c")
    half = columns // 2
    size = iface_sizes
    field, rounded = ((reach, columns), F32), ((reach, columns), BF16)

    heads, = call(heads_kernel, [field], "heads", 2 * reach * width * columns, 2 << 20)(nmat, load)
    heads = passed_along(heads, -1)
    spread, = call(
        functools.partial(tile_kernel, near, far),
        [((near, 2 * tile.shape[0], tile.shape[1] // near), BF16)],
        "tile",
        size=2 << 20,
    )(tile)
    tiles = exchange(spread, ("x", "c"))
    turn = call(turn_kernel, [((reach, width), BF16)] * 2, "turn", 6 * reach**3, 4 << 20)
    n_own, n_away = turn(nmat)
    n_away = passed_along(n_away, -1)
    d_own, d_away = turn(dmat)
    d_away = passed_along(d_away, -1)

    (w_hi, w_lo), (wt_hi, wt_lo) = wave_parts(size[0, 0], directions, reach)

    short = tall = 2 * waves + 8
    flops = 2 * reach * 2 * width * columns

    def pay(rows):
        return ((far, rows, half), F32 if rows == 8 else jnp.int16)

    def solve(payload, extra):
        got = exchange(payload, "z")
        terms, = call(
            functools.partial(coarse_kernel, extra, groups),
            [((groups * near, got.shape[1], half), jnp.int16)],
            "coarse",
            6 * near * 4 * waves * far * waves * columns,
            2 << 20,
        )(tiles, got)
        return exchange(terms, SPREAD)

    def halo(rounded_x):
        return passed_along(rounded_x, 1), passed_along(rounded_x, -1)

    def apply(mode, mats, x, xr, rows, *rest):
        before, after = halo(xr)
        smem = pl.BlockSpec(memory_space=pltpu.SMEM)
        vmem = pl.BlockSpec(memory_space=pltpu.VMEM)
        count = 8 + len(rest)
        return pl.pallas_call(
            functools.partial(apply_kernel, mode),
            out_shape=[
                jax.ShapeDtypeStruct(*field),
                jax.ShapeDtypeStruct(*pay(rows)),
            ],
            in_specs=[smem] + [vmem] * count,
            name="apply_" + mode,
            compiler_params=GRANT,
            cost_estimate=pl.CostEstimate(flops=flops, bytes_accessed=4 << 20, transcendentals=0),
        )(size, mats[0], mats[1], x, xr, before, after, wt_hi, wt_lo, *rest)

    rhs, payload = pl.pallas_call(
        rhs_kernel,
        out_shape=[jax.ShapeDtypeStruct(*field), jax.ShapeDtypeStruct(*pay(short))],
        in_specs=[pl.BlockSpec(memory_space=pltpu.SMEM)]
        + [pl.BlockSpec(memory_space=pltpu.VMEM)] * 5,
        name="rhs",
        compiler_params=GRANT,
    )(size, nmat, load, heads, wt_hi, wt_lo)

    n_mats, d_mats = (n_own, n_away), (d_own, d_away)
    dual, dual_r = call(first_kernel, [field, rounded], "first")(solve(payload, False), w_hi, w_lo)
    res, payload = apply("start", n_mats, dual, dual_r, short, rhs)
    rows, x, xr = call(
        project_kernel, [((waves, columns), F32), field, rounded], "project"
    )(solve(payload, False), w_hi, w_lo, res)
    rho = direction = None
    for step in range(ITERS):
        pre, payload = apply("mid", d_mats, x, xr, tall)
        old = () if step == 0 else (rho, direction)
        rho, direction, dir_r = call(
            functools.partial(search_kernel, step == 0),
            [((8, columns), F32), field, rounded],
            "search",
        )(solve(payload, True), w_hi, w_lo, pre, *old)
        if step < ITERS - 1:
            image, payload = apply("mid", n_mats, direction, dir_r, tall)
            dual, res, x, xr = call(step_kernel, [field, field, field, rounded], "step")(
                solve(payload, True), w_hi, w_lo, rho, direction, image, dual, res, rows
            )
        else:
            image, payload = apply("last", n_mats, direction, dir_r, 8)
            got = exchange(payload, "z")
            terms, = call(partial_kernel, [((groups * near, 8, half), F32)], "partial")(got)
            dual, res = call(final_kernel, [field, field], "final")(
                exchange(terms, SPREAD), rho, direction, image, dual, res
            )
    return dual[None, None], res[None, None]


def solution(mesh):
    finer = Mesh(mesh.devices.reshape(mesh.shape["grp"], 8, 4, 2), ("grp", "z", "x", "c"))
    spec = P("grp", SUB, None, None)
    return jax.shard_map(
        shards,
        mesh=finer,
        in_specs=(spec, spec, spec, spec, P("grp", SUB), P("grp", SUB, None)),
        out_specs=(spec, spec),
        check_vma=False,
    )
```

```python
import functools

import jax
import jax.numpy as jnp
from jax import lax
from jax.experimental import pallas as pl
from jax.experimental.pallas import tpu as pltpu
from jax.sharding import Mesh
from jax.sharding import PartitionSpec as P

NDIR = 64
ITERS = 2
WAVE_NUMBER = 0.785
SUB = ("z", "x", "c")
SPREAD = ("grp", "x", "c")
F32 = jnp.float32
BF16 = jnp.bfloat16
GRANT = pltpu.CompilerParams(vmem_limit_bytes=14 << 20)


def call(body, outs, flops=0, size=0):
    return pl.pallas_call(
        body,
        out_shape=[jax.ShapeDtypeStruct(shape, dtype) for shape, dtype in outs],
        compiler_params=GRANT,
        cost_estimate=pl.CostEstimate(flops=flops, bytes_accessed=size, transcendentals=0),
    )


def mm(a, b):
    return jnp.dot(a, b, preferred_element_type=F32)


def halves(value):
    high = value.astype(BF16)
    return high, (value - high.astype(F32)).astype(BF16)


def mm_wide(pair, value):
    high, low = halves(value)
    return mm(pair[0], high) + (mm(pair[0], low) + mm(pair[1], high))


def reversal(n):
    rows = lax.broadcasted_iota(jnp.int32, (n, n), 0)
    cols = lax.broadcasted_iota(jnp.int32, (n, n), 1)
    return (rows + cols == n - 1).astype(BF16)


def live_rows(size_ref, shape):
    return lax.broadcasted_iota(jnp.int32, shape, 0) < size_ref[0, 0]


def wave_parts(size, directions, reach):
    def basis(axis):
        def along(v):
            return v[:, None] if axis == 0 else v[None, :]

        def across(v):
            return v[None, :] if axis == 0 else v[:, None]

        rows = jnp.arange(reach).astype(F32)
        live = (jnp.arange(reach) < size).astype(F32)
        angle = 2.0 * jnp.pi * directions.astype(F32) / NDIR
        phase = (jnp.arange(directions.shape[0]) % 2).astype(F32) * (jnp.pi / 2.0)
        wave = jnp.cos(WAVE_NUMBER * along(rows) * across(jnp.cos(angle)) + across(phase))
        wave = wave * along(live) / jnp.sqrt(F32(reach))
        high = lax.reduce_precision(wave, 8, 7)
        return high.astype(BF16), (wave - high).astype(BF16)

    return basis(0), basis(1)


STEPS = 14


def exponent(value):
    return jnp.ceil(jnp.log2(jnp.maximum(value, 1e-30)))


def scale_of(power):
    return jnp.exp2(STEPS - power)


def side_by_side(rows):
    half = rows.shape[1] // 2
    return [rows[:, :half], rows[:, half:]]


def coded_sum(extra):
    power = exponent(jnp.abs(extra))
    value = extra * scale_of(power)
    first = jnp.round(value)
    rest = jnp.round((value - first) * 2.0**STEPS)
    return side_by_side(power) + side_by_side(first) + side_by_side(rest)


def pack(blocks, code, out_ref, copies):
    count, waves, columns = blocks.shape
    half = columns // 2
    power = exponent(jnp.max(jnp.abs(blocks), axis=1))
    scaled = jnp.round(blocks * scale_of(power)[:, None, :]).astype(jnp.int32).astype(jnp.int16)
    for k in range(count):
        tail = side_by_side(power[k : k + 1]) + code
        tail = jnp.concatenate(tail, axis=0).astype(jnp.int32).astype(jnp.int16)
        for i in copies[k]:
            out_ref[i, 0:waves] = scaled[k, :, :half]
            out_ref[i, waves : 2 * waves] = scaled[k, :, half:]
            out_ref[i, 2 * waves :] = tail


def no_sum(columns):
    return [jnp.zeros((1, columns // 2), F32)] * 6


def wide(value):
    return value.astype(jnp.int32).astype(F32)


def unpack(value, waves, extra):
    tail = wide(value[2 * waves :])
    back = 1.0 / scale_of(tail[0:4])
    rows = jnp.concatenate(
        [wide(value[0:waves]) * back[0:1], wide(value[waves : 2 * waves]) * back[1:2]], axis=1
    )
    if not extra:
        return rows, None
    sums = (tail[4:6] + tail[6:8] * 2.0**-STEPS) * back[2:4]
    return rows, jnp.concatenate([sums[0:1], sums[1:2]], axis=1)


def coded(value, out_ref):
    rows, columns = value.shape
    power = exponent(jnp.max(jnp.abs(value), axis=0, keepdims=True))
    out_ref[0:rows] = jnp.round(value * scale_of(power)).astype(jnp.int32).astype(jnp.int16)
    power = jnp.broadcast_to(power, (16, columns))
    out_ref[rows:] = power.astype(jnp.int32).astype(jnp.int16)


def decoded(ref):
    value = ref[...]
    rows = value.shape[0] - 16
    return wide(value[0:rows]) * (1.0 / scale_of(wide(value[rows:])[0:1]))


def heads_kernel(mat_ref, loads_ref, out_ref):
    reach = out_ref.shape[0] - 16
    coded(mm(mat_ref[0:reach], loads_ref[...]), out_ref)


def turn_kernel(mat_ref, own_ref, away_ref):
    reach = own_ref.shape[0]
    flip = reversal(reach)
    low = mm(flip, mat_ref[reach:]).astype(BF16)
    own_ref[:, 0:reach] = mm(low[:, reach:], flip).astype(BF16)
    own_ref[:, reach:] = low[:, :reach]
    away_ref[:, 0:reach] = mat_ref[0:reach, 0:reach]
    away_ref[:, reach:] = mm(mat_ref[0:reach, reach:], flip).astype(BF16)


def tile_kernel(near, far, tile_ref, out_ref):
    waves = tile_ref.shape[1] // (near * far)
    value = tile_ref[...]
    for j in range(near):
        pieces = [value[:, (k * near + j) * waves : (k * near + j + 1) * waves] for k in range(far)]
        coded(jnp.concatenate(pieces, axis=1), out_ref.at[j])


def parts_kernel(got_ref, out_ref):
    rows = out_ref.shape[1] // 2
    for j in range(got_ref.shape[0]):
        out_ref[j, 0:rows], out_ref[j, rows:] = halves(decoded(got_ref.at[j]))


def rhs_kernel(size_ref, mat_ref, loads_ref, heads_ref, wt_hi, wt_lo, rhs_ref, pay_ref):
    reach = rhs_ref.shape[0]
    low = mm(mat_ref[reach:], loads_ref[...])
    flip = reversal(reach)
    high_part = low.astype(BF16)
    rest = low - high_part.astype(F32)
    mid_part = rest.astype(BF16)
    low_part = (rest - mid_part.astype(F32)).astype(BF16)
    tails = mm(flip, high_part) + (mm(flip, mid_part) + mm(flip, low_part))
    rhs = jnp.where(live_rows(size_ref, tails.shape), tails - decoded(heads_ref), 0.0)
    rhs_ref[...] = rhs
    rows = mm_wide((wt_hi[...], wt_lo[...]), rhs)
    pack(rows[None], no_sum(rows.shape[1]), pay_ref, [range(pay_ref.shape[0])])


def inner_kernel(own_ref, away_ref, xr_ref, out_ref):
    reach = out_ref.shape[0]
    xr = xr_ref[...]
    out_ref[...] = mm(own_ref[:, 0:reach], xr) + mm(away_ref[:, 0:reach], xr)


def apply_kernel(mode, size_ref, own_ref, away_ref, inner_ref, x_ref, prev_ref, next_ref, wt_hi, wt_lo, *rest):
    reach = inner_ref.shape[0]
    outer = mm(own_ref[:, reach:], prev_ref[...]) + mm(away_ref[:, reach:], next_ref[...])
    product = inner_ref[...] - outer
    product = jnp.where(live_rows(size_ref, product.shape), product, 0.0)
    if mode == "start":
        rhs_ref, out_ref, pay_ref = rest
        product = rhs_ref[...] - product
        extra = None
    else:
        out_ref, pay_ref = rest
        extra = jnp.sum(x_ref[...] * product, axis=0, keepdims=True)
    out_ref[...] = product
    if mode == "last":
        half = extra.shape[1] // 2
        for i in range(pay_ref.shape[0]):
            pay_ref[i, 0:1] = extra[:, :half]
            pay_ref[i, 1:2] = extra[:, half:]
        return
    rows = mm_wide((wt_hi[...], wt_lo[...]), product)
    code = no_sum(rows.shape[1]) if extra is None else coded_sum(extra)
    pack(rows[None], code, pay_ref, [range(pay_ref.shape[0])])


def coarse_kernel(extra, groups, tiles_ref, got_ref, out_ref):
    near, twice, _ = tiles_ref.shape
    height = twice // 2
    waves = height // groups
    far = got_ref.shape[0]
    parts = [unpack(got_ref[k], waves, extra) for k in range(far)]
    stacked = jnp.concatenate([p[0] for p in parts], axis=0)
    if extra:
        code = coded_sum(sum([p[1] for p in parts[1:]], parts[0][1]))
    else:
        code = no_sum(stacked.shape[1])
    high, low = halves(stacked)
    for j in range(near):
        top = tiles_ref[j, 0:height]
        value = mm(top, high) + (mm(top, low) + mm(tiles_ref[j, height:], high))
        blocks = value.reshape(groups, waves, value.shape[1])
        pack(blocks, code, out_ref, [(h * near + j,) for h in range(groups)])


def summed(ref):
    total = ref[0]
    for i in range(1, ref.shape[0]):
        total = total + ref[i]
    return total


def gathered(ref, waves, extra):
    rows, row = unpack(ref[0], waves, extra)
    for i in range(1, ref.shape[0]):
        more, more_row = unpack(ref[i], waves, extra)
        rows = rows + more
        row = row + more_row if extra else None
    return rows, row


def lift(w_hi, w_lo, rows):
    return mm_wide((w_hi[...], w_lo[...]), rows)


def first_kernel(got_ref, w_hi, w_lo, dual_ref, dualr_ref):
    rows, _ = gathered(got_ref, w_hi.shape[1], False)
    dual = lift(w_hi, w_lo, rows)
    dual_ref[...] = dual
    dualr_ref[...] = dual.astype(BF16)


def project_kernel(got_ref, w_hi, w_lo, res_ref, rows_ref, out_ref, outr_ref):
    rows, _ = gathered(got_ref, w_hi.shape[1], False)
    rows_ref[...] = rows
    out = res_ref[...] - lift(w_hi, w_lo, rows)
    out_ref[...] = out
    outr_ref[...] = out.astype(BF16)


def search_kernel(first, got_ref, w_hi, w_lo, pre_ref, *rest):
    rows, rho = gathered(got_ref, w_hi.shape[1], True)
    out = pre_ref[...] - lift(w_hi, w_lo, rows)
    if first:
        rho_ref, out_ref, outr_ref = rest
    else:
        old_rho, old_dir, rho_ref, out_ref, outr_ref = rest
        out = out + rho / old_rho[0:1] * old_dir[...]
    rho_ref[...] = jnp.broadcast_to(rho, rho_ref.shape)
    out_ref[...] = out
    outr_ref[...] = out.astype(BF16)


def step_kernel(got_ref, w_hi, w_lo, rho_ref, dir_ref, img_ref, dual_ref, res_ref, rows_ref,
                new_dual, new_res, new_out, new_outr):
    rows, bottom = gathered(got_ref, w_hi.shape[1], True)
    alpha = rho_ref[0:1] / bottom
    new_dual[...] = dual_ref[...] + alpha * dir_ref[...]
    res = res_ref[...] - alpha * img_ref[...]
    new_res[...] = res
    out = res - lift(w_hi, w_lo, rows_ref[...] - alpha * rows)
    new_out[...] = out
    new_outr[...] = out.astype(BF16)


def partial_kernel(got_ref, out_ref):
    total = summed(got_ref)
    for i in range(out_ref.shape[0]):
        out_ref[i] = total


def final_kernel(got_ref, rho_ref, dir_ref, img_ref, dual_ref, res_ref, new_dual, new_res):
    total = summed(got_ref)
    bottom = jnp.concatenate([total[0:1], total[1:2]], axis=1)
    alpha = rho_ref[0:1] / bottom
    new_dual[...] = dual_ref[...] + alpha * dir_ref[...]
    new_res[...] = res_ref[...] - alpha * img_ref[...]


def passed_along(block, distance):
    n = lax.axis_size(SUB)
    return lax.ppermute(block, SUB, [((i - distance) % n, i) for i in range(n)])


def exchange(value, axes):
    return lax.all_to_all(value, axes, 0, 0, tiled=True)


def shards(neumann, dirichlet, coarse_inverse, loads, iface_sizes, wave_dirs):
    nmat, dmat = neumann[0, 0], dirichlet[0, 0]
    tile, load = coarse_inverse[0, 0], loads[0, 0]
    width, columns = load.shape
    reach = width // 2
    directions = wave_dirs[0, 0]
    waves = directions.shape[0]
    groups = lax.axis_size("grp")
    far = lax.axis_size("z")
    near = lax.axis_size("x") * lax.axis_size("c")
    half = columns // 2
    size = iface_sizes
    field, rounded = ((reach, columns), F32), ((reach, columns), BF16)

    heads, = call(heads_kernel, [((reach + 16, columns), jnp.int16)], 2 * reach * width * columns, 2 << 20)(nmat, load)
    heads = passed_along(heads, -1)
    spread, = call(
        functools.partial(tile_kernel, near, far),
        [((near, tile.shape[0] + 16, tile.shape[1] // near), jnp.int16)],
        size=2 << 20,
    )(tile)
    tiles = exchange(spread, ("x", "c"))
    tiles, = call(
        parts_kernel, [((near, 2 * tile.shape[0], tile.shape[1] // near), BF16)], size=2 << 20
    )(tiles)
    turn = call(turn_kernel, [((reach, width), BF16)] * 2, 6 * reach**3, 4 << 20)
    n_own, n_away = turn(nmat)
    n_away = passed_along(n_away, -1)
    d_own, d_away = turn(dmat)
    d_away = pltpu.with_memory_space_constraint(passed_along(d_away, -1), pltpu.VMEM)

    (w_hi, w_lo), (wt_hi, wt_lo) = wave_parts(size[0, 0], directions, reach)

    short = tall = 2 * waves + 8
    flops = 2 * reach * 2 * width * columns

    def pay(rows):
        return ((far, rows, half), F32 if rows == 8 else jnp.int16)

    def solve(payload, extra):
        got = exchange(payload, "z")
        terms, = call(
            functools.partial(coarse_kernel, extra, groups),
            [((groups * near, got.shape[1], half), jnp.int16)],
            6 * near * 4 * waves * far * waves * columns,
            2 << 20,
        )(tiles, got)
        return exchange(terms, SPREAD)

    def halo(rounded_x):
        return passed_along(rounded_x, 1), passed_along(rounded_x, -1)

    def apply(mode, mats, x, xr, rows, *rest):
        before, after = halo(xr)
        inner, = call(inner_kernel, [field], flops // 2, 1 << 20)(*mats, xr)
        smem = pl.BlockSpec(memory_space=pltpu.SMEM)
        vmem = pl.BlockSpec(memory_space=pltpu.VMEM)
        count = 8 + len(rest)
        return pl.pallas_call(
            functools.partial(apply_kernel, mode),
            out_shape=[
                jax.ShapeDtypeStruct(*field),
                jax.ShapeDtypeStruct(*pay(rows)),
            ],
            in_specs=[smem] + [vmem] * count,
            compiler_params=GRANT,
            cost_estimate=pl.CostEstimate(flops=flops, bytes_accessed=4 << 20, transcendentals=0),
        )(size, mats[0], mats[1], inner, x, before, after, wt_hi, wt_lo, *rest)

    rhs, payload = pl.pallas_call(
        rhs_kernel,
        out_shape=[jax.ShapeDtypeStruct(*field), jax.ShapeDtypeStruct(*pay(short))],
        in_specs=[pl.BlockSpec(memory_space=pltpu.SMEM)]
        + [pl.BlockSpec(memory_space=pltpu.VMEM)] * 5,
        name="rhs",
        compiler_params=GRANT,
    )(size, nmat, load, heads, wt_hi, wt_lo)

    n_mats, d_mats = (n_own, n_away), (d_own, d_away)
    dual, dual_r = call(first_kernel, [field, rounded])(solve(payload, False), w_hi, w_lo)
    res, payload = apply("start", n_mats, dual, dual_r, short, rhs)
    rows, x, xr = call(
        project_kernel, [((waves, columns), F32), field, rounded]
    )(solve(payload, False), w_hi, w_lo, res)
    rho = direction = None
    for step in range(ITERS):
        pre, payload = apply("mid", d_mats, x, xr, tall)
        old = () if step == 0 else (rho, direction)
        rho, direction, dir_r = call(
            functools.partial(search_kernel, step == 0), [((8, columns), F32), field, rounded]
        )(solve(payload, True), w_hi, w_lo, pre, *old)
        if step < ITERS - 1:
            image, payload = apply("mid", n_mats, direction, dir_r, tall)
            dual, res, x, xr = call(step_kernel, [field, field, field, rounded])(
                solve(payload, True), w_hi, w_lo, rho, direction, image, dual, res, rows
            )
        else:
            image, payload = apply("last", n_mats, direction, dir_r, 8)
            got = exchange(payload, "z")
            terms, = call(partial_kernel, [((groups * near, 8, half), F32)])(got)
            dual, res = call(final_kernel, [field, field])(
                exchange(terms, SPREAD), rho, direction, image, dual, res
            )
    return dual[None, None], res[None, None]


def solution(mesh):
    finer = Mesh(mesh.devices.reshape(mesh.shape["grp"], 8, 4, 2), ("grp", "z", "x", "c"))
    spec = P("grp", SUB, None, None)

    return jax.shard_map(
        shards,
        mesh=finer,
        in_specs=(spec, spec, spec, spec, P("grp", SUB), P("grp", SUB, None)),
        out_specs=(spec, spec),
        check_vma=False,
    )
```

```python
import functools

import jax
import jax.numpy as jnp
from jax import lax
from jax.experimental import pallas as pl
from jax.experimental.pallas import tpu as pltpu
from jax.sharding import Mesh
from jax.sharding import PartitionSpec as P

NDIR = 64
ITERS = 2
WAVE_NUMBER = 0.785
SUB = ("z", "x", "c")
GATHER = ("z", "c")
SPREAD = ("grp", "x")
F32 = jnp.float32
BF16 = jnp.bfloat16
GRANT = pltpu.CompilerParams(vmem_limit_bytes=14 << 20)


def call(body, outs, flops=0, size=0):
    return pl.pallas_call(
        body,
        out_shape=[jax.ShapeDtypeStruct(shape, dtype) for shape, dtype in outs],
        compiler_params=GRANT,
        cost_estimate=pl.CostEstimate(flops=flops, bytes_accessed=size, transcendentals=0),
    )


def mm(a, b):
    return jnp.dot(a, b, preferred_element_type=F32)


def halves(value):
    high = value.astype(BF16)
    return high, (value - high.astype(F32)).astype(BF16)


def mm_wide(pair, value):
    high, low = halves(value)
    return mm(pair[0], high) + (mm(pair[0], low) + mm(pair[1], high))


def reversal(n):
    rows = lax.broadcasted_iota(jnp.int32, (n, n), 0)
    cols = lax.broadcasted_iota(jnp.int32, (n, n), 1)
    return (rows + cols == n - 1).astype(BF16)


def live_rows(size_ref, shape):
    return lax.broadcasted_iota(jnp.int32, shape, 0) < size_ref[0, 0]


def wave_parts(size, directions, reach):
    def basis(axis):
        def along(v):
            return v[:, None] if axis == 0 else v[None, :]

        def across(v):
            return v[None, :] if axis == 0 else v[:, None]

        rows = jnp.arange(reach).astype(F32)
        live = (jnp.arange(reach) < size).astype(F32)
        angle = 2.0 * jnp.pi * directions.astype(F32) / NDIR
        phase = (jnp.arange(directions.shape[0]) % 2).astype(F32) * (jnp.pi / 2.0)
        wave = jnp.cos(WAVE_NUMBER * along(rows) * across(jnp.cos(angle)) + across(phase))
        wave = wave * along(live) / jnp.sqrt(F32(reach))
        high = lax.reduce_precision(wave, 8, 7)
        return high.astype(BF16), (wave - high).astype(BF16)

    return basis(0), basis(1)


STEPS = 14


def exponent(value):
    return jnp.ceil(jnp.log2(jnp.maximum(value, 1e-30)))


def scale_of(power):
    return jnp.exp2(STEPS - power)


def side_by_side(rows):
    half = rows.shape[1] // 2
    return [rows[:, :half], rows[:, half:]]


def coded_sum(extra):
    power = exponent(jnp.abs(extra))
    value = extra * scale_of(power)
    first = jnp.round(value)
    rest = jnp.round((value - first) * 2.0**STEPS)
    return side_by_side(power) + side_by_side(first) + side_by_side(rest)


def pack(blocks, code, out_ref, copies):
    count, waves, columns = blocks.shape
    half = columns // 2
    power = exponent(jnp.max(jnp.abs(blocks), axis=1))
    scaled = jnp.round(blocks * scale_of(power)[:, None, :]).astype(jnp.int32).astype(jnp.int16)
    for k in range(count):
        tail = side_by_side(power[k : k + 1]) + code
        tail = jnp.concatenate(tail, axis=0).astype(jnp.int32).astype(jnp.int16)
        for i in copies[k]:
            out_ref[i, 0:waves] = scaled[k, :, :half]
            out_ref[i, waves : 2 * waves] = scaled[k, :, half:]
            out_ref[i, 2 * waves :] = tail


def no_sum(columns):
    return [jnp.zeros((1, columns // 2), F32)] * 6


def wide(value):
    return value.astype(jnp.int32).astype(F32)


def unpack(value, waves, extra):
    tail = wide(value[2 * waves :])
    back = 1.0 / scale_of(tail[0:4])
    rows = jnp.concatenate(
        [wide(value[0:waves]) * back[0:1], wide(value[waves : 2 * waves]) * back[1:2]], axis=1
    )
    if not extra:
        return rows, None
    sums = (tail[4:6] + tail[6:8] * 2.0**-STEPS) * back[2:4]
    return rows, jnp.concatenate([sums[0:1], sums[1:2]], axis=1)


def coded(value, out_ref):
    rows, columns = value.shape
    power = exponent(jnp.max(jnp.abs(value), axis=0, keepdims=True))
    out_ref[0:rows] = jnp.round(value * scale_of(power)).astype(jnp.int32).astype(jnp.int16)
    power = jnp.broadcast_to(power, (16, columns))
    out_ref[rows:] = power.astype(jnp.int32).astype(jnp.int16)


def decoded(ref):
    value = ref[...]
    rows = value.shape[0] - 16
    return wide(value[0:rows]) * (1.0 / scale_of(wide(value[rows:])[0:1]))


def heads_kernel(mat_ref, loads_ref, out_ref):
    reach = out_ref.shape[0] - 16
    coded(mm(mat_ref[0:reach], loads_ref[...]), out_ref)


def turn_kernel(mat_ref, own_ref, away_ref):
    reach = own_ref.shape[0]
    flip = reversal(reach)
    low = mm(flip, mat_ref[reach:]).astype(BF16)
    own_ref[:, 0:reach] = mm(low[:, reach:], flip).astype(BF16)
    own_ref[:, reach:] = low[:, :reach]
    away_ref[:, 0:reach] = mat_ref[0:reach, 0:reach]
    away_ref[:, reach:] = mm(mat_ref[0:reach, reach:], flip).astype(BF16)


def tile_kernel(near, far, tile_ref, out_ref):
    waves = tile_ref.shape[1] // (near * far)
    value = tile_ref[...]
    for j in range(near):
        pieces = [value[:, (k * near + j) * waves : (k * near + j + 1) * waves] for k in range(far)]
        coded(jnp.concatenate(pieces, axis=1), out_ref.at[j])


def parts_kernel(got_ref, out_ref):
    rows = out_ref.shape[1] // 2
    for j in range(got_ref.shape[0]):
        out_ref[j, 0:rows], out_ref[j, rows:] = halves(decoded(got_ref.at[j]))


def rhs_kernel(size_ref, mat_ref, loads_ref, heads_ref, wt_hi, wt_lo, rhs_ref, pay_ref):
    reach = rhs_ref.shape[0]
    low = mm(mat_ref[reach:], loads_ref[...])
    flip = reversal(reach)
    high_part = low.astype(BF16)
    rest = low - high_part.astype(F32)
    mid_part = rest.astype(BF16)
    low_part = (rest - mid_part.astype(F32)).astype(BF16)
    tails = mm(flip, high_part) + (mm(flip, mid_part) + mm(flip, low_part))
    rhs = jnp.where(live_rows(size_ref, tails.shape), tails - decoded(heads_ref), 0.0)
    rhs_ref[...] = rhs
    rows = mm_wide((wt_hi[...], wt_lo[...]), rhs)
    pack(rows[None], no_sum(rows.shape[1]), pay_ref, [range(pay_ref.shape[0])])


def inner_kernel(own_ref, away_ref, xr_ref, out_ref):
    reach = out_ref.shape[0]
    xr = xr_ref[...]
    out_ref[...] = mm(own_ref[:, 0:reach], xr) + mm(away_ref[:, 0:reach], xr)


def apply_kernel(mode, size_ref, own_ref, away_ref, inner_ref, x_ref, prev_ref, next_ref, wt_hi, wt_lo, *rest):
    reach = inner_ref.shape[0]
    outer = mm(own_ref[:, reach:], prev_ref[...]) + mm(away_ref[:, reach:], next_ref[...])
    product = inner_ref[...] - outer
    product = jnp.where(live_rows(size_ref, product.shape), product, 0.0)
    if mode == "start":
        rhs_ref, out_ref, pay_ref = rest
        product = rhs_ref[...] - product
        extra = None
    else:
        out_ref, pay_ref = rest
        extra = jnp.sum(x_ref[...] * product, axis=0, keepdims=True)
    out_ref[...] = product
    if mode == "last":
        half = extra.shape[1] // 2
        for i in range(pay_ref.shape[0]):
            pay_ref[i, 0:1] = extra[:, :half]
            pay_ref[i, 1:2] = extra[:, half:]
        return
    rows = mm_wide((wt_hi[...], wt_lo[...]), product)
    code = no_sum(rows.shape[1]) if extra is None else coded_sum(extra)
    pack(rows[None], code, pay_ref, [range(pay_ref.shape[0])])


def coarse_kernel(extra, groups, tiles_ref, got_ref, out_ref):
    near, twice, _ = tiles_ref.shape
    height = twice // 2
    waves = height // groups
    far = got_ref.shape[0]
    parts = [unpack(got_ref[k], waves, extra) for k in range(far)]
    stacked = jnp.concatenate([p[0] for p in parts], axis=0)
    if extra:
        code = coded_sum(sum([p[1] for p in parts[1:]], parts[0][1]))
    else:
        code = no_sum(stacked.shape[1])
    high, low = halves(stacked)
    for j in range(near):
        top = tiles_ref[j, 0:height]
        value = mm(top, high) + (mm(top, low) + mm(tiles_ref[j, height:], high))
        blocks = value.reshape(groups, waves, value.shape[1])
        pack(blocks, code, out_ref, [(h * near + j,) for h in range(groups)])


def summed(ref):
    total = ref[0]
    for i in range(1, ref.shape[0]):
        total = total + ref[i]
    return total


def gathered(ref, waves, extra):
    rows, row = unpack(ref[0], waves, extra)
    for i in range(1, ref.shape[0]):
        more, more_row = unpack(ref[i], waves, extra)
        rows = rows + more
        row = row + more_row if extra else None
    return rows, row


def lift(w_hi, w_lo, rows):
    return mm_wide((w_hi[...], w_lo[...]), rows)


def first_kernel(got_ref, w_hi, w_lo, dual_ref, dualr_ref):
    rows, _ = gathered(got_ref, w_hi.shape[1], False)
    dual = lift(w_hi, w_lo, rows)
    dual_ref[...] = dual
    dualr_ref[...] = dual.astype(BF16)


def project_kernel(got_ref, w_hi, w_lo, res_ref, rows_ref, out_ref, outr_ref):
    rows, _ = gathered(got_ref, w_hi.shape[1], False)
    rows_ref[...] = rows
    out = res_ref[...] - lift(w_hi, w_lo, rows)
    out_ref[...] = out
    outr_ref[...] = out.astype(BF16)


def search_kernel(first, got_ref, w_hi, w_lo, pre_ref, *rest):
    rows, rho = gathered(got_ref, w_hi.shape[1], True)
    out = pre_ref[...] - lift(w_hi, w_lo, rows)
    if first:
        rho_ref, out_ref, outr_ref = rest
    else:
        old_rho, old_dir, rho_ref, out_ref, outr_ref = rest
        out = out + rho / old_rho[0:1] * old_dir[...]
    rho_ref[...] = jnp.broadcast_to(rho, rho_ref.shape)
    out_ref[...] = out
    outr_ref[...] = out.astype(BF16)


def step_kernel(got_ref, w_hi, w_lo, rho_ref, dir_ref, img_ref, dual_ref, res_ref, rows_ref,
                new_dual, new_res, new_out, new_outr):
    rows, bottom = gathered(got_ref, w_hi.shape[1], True)
    alpha = rho_ref[0:1] / bottom
    new_dual[...] = dual_ref[...] + alpha * dir_ref[...]
    res = res_ref[...] - alpha * img_ref[...]
    new_res[...] = res
    out = res - lift(w_hi, w_lo, rows_ref[...] - alpha * rows)
    new_out[...] = out
    new_outr[...] = out.astype(BF16)


def partial_kernel(got_ref, out_ref):
    total = summed(got_ref)
    for i in range(out_ref.shape[0]):
        out_ref[i] = total


def final_kernel(got_ref, rho_ref, dir_ref, img_ref, dual_ref, res_ref, new_dual, new_res):
    total = summed(got_ref)
    bottom = jnp.concatenate([total[0:1], total[1:2]], axis=1)
    alpha = rho_ref[0:1] / bottom
    new_dual[...] = dual_ref[...] + alpha * dir_ref[...]
    new_res[...] = res_ref[...] - alpha * img_ref[...]


def passed_along(block, distance):
    n = lax.axis_size(SUB)
    return lax.ppermute(block, SUB, [((i - distance) % n, i) for i in range(n)])


def exchange(value, axes):
    return lax.all_to_all(value, axes, 0, 0, tiled=True)


def shards(neumann, dirichlet, coarse_inverse, loads, iface_sizes, wave_dirs):
    nmat, dmat = neumann[0, 0], dirichlet[0, 0]
    tile, load = coarse_inverse[0, 0], loads[0, 0]
    width, columns = load.shape
    reach = width // 2
    directions = wave_dirs[0, 0]
    waves = directions.shape[0]
    groups = lax.axis_size("grp")
    near = lax.axis_size("x")
    far = lax.axis_size(GATHER)
    half = columns // 2
    size = iface_sizes
    field, rounded = ((reach, columns), F32), ((reach, columns), BF16)

    heads, = call(heads_kernel, [((reach + 16, columns), jnp.int16)], 2 * reach * width * columns, 2 << 20)(nmat, load)
    heads = passed_along(heads, -1)
    spread, = call(
        functools.partial(tile_kernel, near, lax.axis_size("z")),
        [((near, tile.shape[0] + 16, tile.shape[1] // near), jnp.int16)],
        size=2 << 20,
    )(tile)
    tiles = exchange(spread, "x")
    tiles, = call(
        parts_kernel, [((near, 2 * tile.shape[0], tile.shape[1] // near), BF16)], size=2 << 20
    )(tiles)
    turn = call(turn_kernel, [((reach, width), BF16)] * 2, 6 * reach**3, 4 << 20)
    n_own, n_away = turn(nmat)
    n_away = passed_along(n_away, -1)
    d_own, d_away = turn(dmat)
    d_away = pltpu.with_memory_space_constraint(passed_along(d_away, -1), pltpu.VMEM)

    (w_hi, w_lo), (wt_hi, wt_lo) = wave_parts(size[0, 0], directions, reach)

    short = tall = 2 * waves + 8
    flops = 2 * reach * 2 * width * columns

    def pay(rows):
        return ((far, rows, half), F32 if rows == 8 else jnp.int16)

    def solve(payload, extra):
        got = exchange(payload, GATHER)
        terms, = call(
            functools.partial(coarse_kernel, extra, groups),
            [((groups * near, got.shape[1], half), jnp.int16)],
            6 * near * 4 * waves * far * waves * columns,
            2 << 20,
        )(tiles, got)
        return exchange(terms, SPREAD)

    def halo(rounded_x):
        return passed_along(rounded_x, 1), passed_along(rounded_x, -1)

    def apply(mode, mats, x, xr, rows, *rest):
        before, after = halo(xr)
        inner, = call(inner_kernel, [field], flops // 2, 1 << 20)(*mats, xr)
        smem = pl.BlockSpec(memory_space=pltpu.SMEM)
        vmem = pl.BlockSpec(memory_space=pltpu.VMEM)
        count = 8 + len(rest)
        return pl.pallas_call(
            functools.partial(apply_kernel, mode),
            out_shape=[
                jax.ShapeDtypeStruct(*field),
                jax.ShapeDtypeStruct(*pay(rows)),
            ],
            in_specs=[smem] + [vmem] * count,
            compiler_params=GRANT,
            cost_estimate=pl.CostEstimate(flops=flops, bytes_accessed=4 << 20, transcendentals=0),
        )(size, mats[0], mats[1], inner, x, before, after, wt_hi, wt_lo, *rest)

    rhs, payload = pl.pallas_call(
        rhs_kernel,
        out_shape=[jax.ShapeDtypeStruct(*field), jax.ShapeDtypeStruct(*pay(short))],
        in_specs=[pl.BlockSpec(memory_space=pltpu.SMEM)]
        + [pl.BlockSpec(memory_space=pltpu.VMEM)] * 5,
        name="rhs",
        compiler_params=GRANT,
    )(size, nmat, load, heads, wt_hi, wt_lo)

    n_mats, d_mats = (n_own, n_away), (d_own, d_away)
    dual, dual_r = call(first_kernel, [field, rounded])(solve(payload, False), w_hi, w_lo)
    res, payload = apply("start", n_mats, dual, dual_r, short, rhs)
    rows, x, xr = call(
        project_kernel, [((waves, columns), F32), field, rounded]
    )(solve(payload, False), w_hi, w_lo, res)
    rho = direction = None
    for step in range(ITERS):
        pre, payload = apply("mid", d_mats, x, xr, tall)
        old = () if step == 0 else (rho, direction)
        rho, direction, dir_r = call(
            functools.partial(search_kernel, step == 0), [((8, columns), F32), field, rounded]
        )(solve(payload, True), w_hi, w_lo, pre, *old)
        if step < ITERS - 1:
            image, payload = apply("mid", n_mats, direction, dir_r, tall)
            dual, res, x, xr = call(step_kernel, [field, field, field, rounded])(
                solve(payload, True), w_hi, w_lo, rho, direction, image, dual, res, rows
            )
        else:
            image, payload = apply("last", n_mats, direction, dir_r, 8)
            got = exchange(payload, GATHER)
            terms, = call(partial_kernel, [((groups * near, 8, half), F32)])(got)
            dual, res = call(final_kernel, [field, field])(
                exchange(terms, SPREAD), rho, direction, image, dual, res
            )
    return dual[None, None], res[None, None]


def solution(mesh):
    finer = Mesh(mesh.devices.reshape(mesh.shape["grp"], 8, 4, 2), ("grp", "z", "x", "c"))
    spec = P("grp", SUB, None, None)

    return jax.shard_map(
        shards,
        mesh=finer,
        in_specs=(spec, spec, spec, spec, P("grp", SUB), P("grp", SUB, None)),
        out_specs=(spec, spec),
        check_vma=False,
    )
```

```python
import functools

import jax
import jax.numpy as jnp
from jax import lax
from jax.experimental import pallas as pl
from jax.experimental.pallas import tpu as pltpu
from jax.sharding import Mesh
from jax.sharding import PartitionSpec as P

NDIR = 64
ITERS = 2
WAVE_NUMBER = 0.785
SUB = ("z", "x", "c")
GATHER = ("z", "c")
SPREAD = ("grp", "x")
F32 = jnp.float32
BF16 = jnp.bfloat16
GRANT = pltpu.CompilerParams(vmem_limit_bytes=14 << 20)


def call(body, outs, flops=0, size=0):
    return pl.pallas_call(
        body,
        out_shape=[jax.ShapeDtypeStruct(shape, dtype) for shape, dtype in outs],
        compiler_params=GRANT,
        cost_estimate=pl.CostEstimate(flops=flops, bytes_accessed=size, transcendentals=0),
    )


def mm(a, b):
    return jnp.dot(a, b, preferred_element_type=F32)


def halves(value):
    high = value.astype(BF16)
    return high, (value - high.astype(F32)).astype(BF16)


def mm_wide(pair, value):
    high, low = halves(value)
    return mm(pair[0], high) + (mm(pair[0], low) + mm(pair[1], high))


def reversal(n):
    rows = lax.broadcasted_iota(jnp.int32, (n, n), 0)
    cols = lax.broadcasted_iota(jnp.int32, (n, n), 1)
    return (rows + cols == n - 1).astype(BF16)


def live_rows(size_ref, shape):
    return lax.broadcasted_iota(jnp.int32, shape, 0) < size_ref[0, 0]


def wave_parts(size, directions, reach):
    def basis(axis):
        def along(v):
            return v[:, None] if axis == 0 else v[None, :]

        def across(v):
            return v[None, :] if axis == 0 else v[:, None]

        rows = jnp.arange(reach).astype(F32)
        live = (jnp.arange(reach) < size).astype(F32)
        angle = 2.0 * jnp.pi * directions.astype(F32) / NDIR
        phase = (jnp.arange(directions.shape[0]) % 2).astype(F32) * (jnp.pi / 2.0)
        wave = jnp.cos(WAVE_NUMBER * along(rows) * across(jnp.cos(angle)) + across(phase))
        wave = wave * along(live) / jnp.sqrt(F32(reach))
        high = lax.reduce_precision(wave, 8, 7)
        return high.astype(BF16), (wave - high).astype(BF16)

    return basis(0), basis(1)


STEPS = 14


def exponent(value):
    return jnp.ceil(jnp.log2(jnp.maximum(value, 1e-30)))


def scale_of(power):
    return jnp.exp2(STEPS - power)


def side_by_side(rows):
    half = rows.shape[1] // 2
    return [rows[:, :half], rows[:, half:]]


def coded_sum(extra):
    power = exponent(jnp.abs(extra))
    value = extra * scale_of(power)
    first = jnp.round(value)
    rest = jnp.round((value - first) * 2.0**STEPS)
    return side_by_side(power) + side_by_side(first) + side_by_side(rest)


def pack(blocks, code, out_ref, copies):
    count, waves, columns = blocks.shape
    half = columns // 2
    power = exponent(jnp.max(jnp.abs(blocks), axis=1))
    scaled = jnp.round(blocks * scale_of(power)[:, None, :]).astype(jnp.int32).astype(jnp.int16)
    for k in range(count):
        tail = side_by_side(power[k : k + 1]) + code
        tail = jnp.concatenate(tail, axis=0).astype(jnp.int32).astype(jnp.int16)
        for i in copies[k]:
            out_ref[i, 0:waves] = scaled[k, :, :half]
            out_ref[i, waves : 2 * waves] = scaled[k, :, half:]
            out_ref[i, 2 * waves :] = tail


def no_sum(columns):
    return [jnp.zeros((1, columns // 2), F32)] * 6


def wide(value):
    return value.astype(jnp.int32).astype(F32)


def unpack(value, waves, extra):
    tail = wide(value[2 * waves :])
    back = 1.0 / scale_of(tail[0:4])
    rows = jnp.concatenate(
        [wide(value[0:waves]) * back[0:1], wide(value[waves : 2 * waves]) * back[1:2]], axis=1
    )
    if not extra:
        return rows, None
    sums = (tail[4:6] + tail[6:8] * 2.0**-STEPS) * back[2:4]
    return rows, jnp.concatenate([sums[0:1], sums[1:2]], axis=1)


def coded(value, out_ref):
    rows, columns = value.shape
    power = exponent(jnp.max(jnp.abs(value), axis=0, keepdims=True))
    out_ref[0:rows] = jnp.round(value * scale_of(power)).astype(jnp.int32).astype(jnp.int16)
    power = jnp.broadcast_to(power, (16, columns))
    out_ref[rows:] = power.astype(jnp.int32).astype(jnp.int16)


def decoded(ref):
    value = ref[...]
    rows = value.shape[0] - 16
    return wide(value[0:rows]) * (1.0 / scale_of(wide(value[rows:])[0:1]))


def heads_kernel(mat_ref, loads_ref, out_ref):
    reach = out_ref.shape[0] - 16
    coded(mm(mat_ref[0:reach], loads_ref[...]), out_ref)


def turn_kernel(mat_ref, own_ref, away_ref):
    reach = own_ref.shape[0]
    flip = reversal(reach)
    low = mm(flip, mat_ref[reach:]).astype(BF16)
    own_ref[:, 0:reach] = mm(low[:, reach:], flip).astype(BF16)
    own_ref[:, reach:] = low[:, :reach]
    away_ref[:, 0:reach] = mat_ref[0:reach, 0:reach]
    away_ref[:, reach:] = mm(mat_ref[0:reach, reach:], flip).astype(BF16)


def tile_kernel(near, far, place_ref, tile_ref, out_ref, *rest):
    *away_refs, all_ref = rest
    place = place_ref[0, 0]
    waves = tile_ref.shape[1] // (near * far)
    value = tile_ref[...]
    for j in range(near):
        pieces = [value[:, (k * near + j) * waves : (k * near + j + 1) * waves] for k in range(far)]
        coded(jnp.concatenate(pieces, axis=1), all_ref.at[lax.rem(j + near - place, near)])
    for d, ref in enumerate((out_ref, *away_refs)):
        ref[...] = all_ref[d]


def parts_kernel(place_ref, *refs):
    *got_refs, out_ref = refs
    near = len(got_refs)
    rows = out_ref.shape[1] // 2
    for d, ref in enumerate(got_refs):
        source = lax.rem(place_ref[0, 0] + near - d, near)
        high, low = halves(decoded(ref))
        out_ref[source, 0:rows] = high
        out_ref[source, rows:] = low


def rhs_kernel(size_ref, mat_ref, loads_ref, heads_ref, wt_hi, wt_lo, rhs_ref, pay_ref):
    reach = rhs_ref.shape[0]
    low = mm(mat_ref[reach:], loads_ref[...])
    flip = reversal(reach)
    high_part = low.astype(BF16)
    rest = low - high_part.astype(F32)
    mid_part = rest.astype(BF16)
    low_part = (rest - mid_part.astype(F32)).astype(BF16)
    tails = mm(flip, high_part) + (mm(flip, mid_part) + mm(flip, low_part))
    rhs = jnp.where(live_rows(size_ref, tails.shape), tails - decoded(heads_ref), 0.0)
    rhs_ref[...] = rhs
    rows = mm_wide((wt_hi[...], wt_lo[...]), rhs)
    pack(rows[None], no_sum(rows.shape[1]), pay_ref, [range(pay_ref.shape[0])])


def inner_kernel(own_ref, away_ref, xr_ref, out_ref):
    reach = out_ref.shape[0]
    xr = xr_ref[...]
    out_ref[...] = mm(own_ref[:, 0:reach], xr) + mm(away_ref[:, 0:reach], xr)


def apply_kernel(mode, size_ref, own_ref, away_ref, inner_ref, x_ref, prev_ref, next_ref, wt_hi, wt_lo, *rest):
    reach = inner_ref.shape[0]
    outer = mm(own_ref[:, reach:], prev_ref[...]) + mm(away_ref[:, reach:], next_ref[...])
    product = inner_ref[...] - outer
    product = jnp.where(live_rows(size_ref, product.shape), product, 0.0)
    if mode == "start":
        rhs_ref, out_ref, pay_ref = rest
        product = rhs_ref[...] - product
        extra = None
    else:
        out_ref, pay_ref = rest
        extra = jnp.sum(x_ref[...] * product, axis=0, keepdims=True)
    out_ref[...] = product
    if mode == "last":
        half = extra.shape[1] // 2
        for i in range(pay_ref.shape[0]):
            pay_ref[i, 0:1] = extra[:, :half]
            pay_ref[i, 1:2] = extra[:, half:]
        return
    rows = mm_wide((wt_hi[...], wt_lo[...]), product)
    code = no_sum(rows.shape[1]) if extra is None else coded_sum(extra)
    pack(rows[None], code, pay_ref, [range(pay_ref.shape[0])])


def coarse_kernel(extra, groups, tiles_ref, got_ref, out_ref):
    near, twice, _ = tiles_ref.shape
    height = twice // 2
    waves = height // groups
    far = got_ref.shape[0]
    parts = [unpack(got_ref[k], waves, extra) for k in range(far)]
    stacked = jnp.concatenate([p[0] for p in parts], axis=0)
    if extra:
        code = coded_sum(sum([p[1] for p in parts[1:]], parts[0][1]))
    else:
        code = no_sum(stacked.shape[1])
    high, low = halves(stacked)
    for j in range(near):
        top = tiles_ref[j, 0:height]
        value = mm(top, high) + (mm(top, low) + mm(tiles_ref[j, height:], high))
        blocks = value.reshape(groups, waves, value.shape[1])
        pack(blocks, code, out_ref, [(h * near + j,) for h in range(groups)])


def summed(ref):
    total = ref[0]
    for i in range(1, ref.shape[0]):
        total = total + ref[i]
    return total


def gathered(ref, waves, extra):
    rows, row = unpack(ref[0], waves, extra)
    for i in range(1, ref.shape[0]):
        more, more_row = unpack(ref[i], waves, extra)
        rows = rows + more
        row = row + more_row if extra else None
    return rows, row


def lift(w_hi, w_lo, rows):
    return mm_wide((w_hi[...], w_lo[...]), rows)


def first_kernel(got_ref, w_hi, w_lo, dual_ref, dualr_ref):
    rows, _ = gathered(got_ref, w_hi.shape[1], False)
    dual = lift(w_hi, w_lo, rows)
    dual_ref[...] = dual
    dualr_ref[...] = dual.astype(BF16)


def project_kernel(got_ref, w_hi, w_lo, res_ref, rows_ref, out_ref, outr_ref):
    rows, _ = gathered(got_ref, w_hi.shape[1], False)
    rows_ref[...] = rows
    out = res_ref[...] - lift(w_hi, w_lo, rows)
    out_ref[...] = out
    outr_ref[...] = out.astype(BF16)


def search_kernel(first, got_ref, w_hi, w_lo, pre_ref, *rest):
    rows, rho = gathered(got_ref, w_hi.shape[1], True)
    out = pre_ref[...] - lift(w_hi, w_lo, rows)
    if first:
        rho_ref, out_ref, outr_ref = rest
    else:
        old_rho, old_dir, rho_ref, out_ref, outr_ref = rest
        out = out + rho / old_rho[0:1] * old_dir[...]
    rho_ref[...] = jnp.broadcast_to(rho, rho_ref.shape)
    out_ref[...] = out
    outr_ref[...] = out.astype(BF16)


def step_kernel(got_ref, w_hi, w_lo, rho_ref, dir_ref, img_ref, dual_ref, res_ref, rows_ref,
                new_dual, new_res, new_out, new_outr):
    rows, bottom = gathered(got_ref, w_hi.shape[1], True)
    alpha = rho_ref[0:1] / bottom
    new_dual[...] = dual_ref[...] + alpha * dir_ref[...]
    res = res_ref[...] - alpha * img_ref[...]
    new_res[...] = res
    out = res - lift(w_hi, w_lo, rows_ref[...] - alpha * rows)
    new_out[...] = out
    new_outr[...] = out.astype(BF16)


def partial_kernel(got_ref, out_ref):
    total = summed(got_ref)
    for i in range(out_ref.shape[0]):
        out_ref[i] = total


def final_kernel(got_ref, rho_ref, dir_ref, img_ref, dual_ref, res_ref, new_dual, new_res):
    total = summed(got_ref)
    bottom = jnp.concatenate([total[0:1], total[1:2]], axis=1)
    alpha = rho_ref[0:1] / bottom
    new_dual[...] = dual_ref[...] + alpha * dir_ref[...]
    new_res[...] = res_ref[...] - alpha * img_ref[...]


def passed_along(block, distance):
    n = lax.axis_size(SUB)
    return lax.ppermute(block, SUB, [((i - distance) % n, i) for i in range(n)])


def exchange(value, axes):
    return lax.all_to_all(value, axes, 0, 0, tiled=True)


def shards(neumann, dirichlet, coarse_inverse, loads, iface_sizes, wave_dirs):
    nmat, dmat = neumann[0, 0], dirichlet[0, 0]
    tile, load = coarse_inverse[0, 0], loads[0, 0]
    width, columns = load.shape
    reach = width // 2
    directions = wave_dirs[0, 0]
    waves = directions.shape[0]
    groups = lax.axis_size("grp")
    near = lax.axis_size("x")
    far = lax.axis_size(GATHER)
    half = columns // 2
    size = iface_sizes
    field, rounded = ((reach, columns), F32), ((reach, columns), BF16)

    heads, = call(heads_kernel, [((reach + 16, columns), jnp.int16)], 2 * reach * width * columns, 2 << 20)(nmat, load)
    heads = passed_along(heads, -1)
    place = lax.axis_index("x").astype(jnp.int32).reshape(1, 1)
    smem = pl.BlockSpec(memory_space=pltpu.SMEM)
    vmem = pl.BlockSpec(memory_space=pltpu.VMEM)
    block = ((tile.shape[0] + 16, tile.shape[1] // near), jnp.int16)
    kept, *sent = pl.pallas_call(
        functools.partial(tile_kernel, near, lax.axis_size("z")),
        out_shape=[jax.ShapeDtypeStruct(*block)] * near,
        in_specs=[smem, vmem],
        scratch_shapes=[pltpu.VMEM((near, *block[0]), block[1])],
        name="tile",
        compiler_params=GRANT,
    )(place, tile)
    came = [
        lax.ppermute(sent[d - 1], "x", [(i, (i + d) % near) for i in range(near)])
        for d in range(1, near)
    ]
    tiles = pl.pallas_call(
        parts_kernel,
        out_shape=jax.ShapeDtypeStruct((near, 2 * tile.shape[0], tile.shape[1] // near), BF16),
        in_specs=[smem] + [vmem] * near,
        name="parts",
        compiler_params=GRANT,
    )(place, kept, *came)
    turn = call(turn_kernel, [((reach, width), BF16)] * 2, 6 * reach**3, 4 << 20)
    n_own, n_away = turn(nmat)
    n_away = passed_along(n_away, -1)
    d_own, d_away = turn(dmat)
    d_away = pltpu.with_memory_space_constraint(passed_along(d_away, -1), pltpu.VMEM)

    (w_hi, w_lo), (wt_hi, wt_lo) = wave_parts(size[0, 0], directions, reach)

    short = tall = 2 * waves + 8
    flops = 2 * reach * 2 * width * columns

    def pay(rows):
        return ((far, rows, half), F32 if rows == 8 else jnp.int16)

    def solve(payload, extra):
        got = exchange(payload, GATHER)
        terms, = call(
            functools.partial(coarse_kernel, extra, groups),
            [((groups * near, got.shape[1], half), jnp.int16)],
            6 * near * 4 * waves * far * waves * columns,
            2 << 20,
        )(tiles, got)
        return exchange(terms, SPREAD)

    def halo(rounded_x):
        return passed_along(rounded_x, 1), passed_along(rounded_x, -1)

    def apply(mode, mats, x, xr, rows, *rest):
        before, after = halo(xr)
        inner, = call(inner_kernel, [field], flops // 2, 1 << 20)(*mats, xr)
        smem = pl.BlockSpec(memory_space=pltpu.SMEM)
        vmem = pl.BlockSpec(memory_space=pltpu.VMEM)
        count = 8 + len(rest)
        return pl.pallas_call(
            functools.partial(apply_kernel, mode),
            out_shape=[
                jax.ShapeDtypeStruct(*field),
                jax.ShapeDtypeStruct(*pay(rows)),
            ],
            in_specs=[smem] + [vmem] * count,
            compiler_params=GRANT,
            cost_estimate=pl.CostEstimate(flops=flops, bytes_accessed=4 << 20, transcendentals=0),
        )(size, mats[0], mats[1], inner, x, before, after, wt_hi, wt_lo, *rest)

    rhs, payload = pl.pallas_call(
        rhs_kernel,
        out_shape=[jax.ShapeDtypeStruct(*field), jax.ShapeDtypeStruct(*pay(short))],
        in_specs=[pl.BlockSpec(memory_space=pltpu.SMEM)]
        + [pl.BlockSpec(memory_space=pltpu.VMEM)] * 5,
        name="rhs",
        compiler_params=GRANT,
    )(size, nmat, load, heads, wt_hi, wt_lo)

    n_mats, d_mats = (n_own, n_away), (d_own, d_away)
    dual, dual_r = call(first_kernel, [field, rounded])(solve(payload, False), w_hi, w_lo)
    res, payload = apply("start", n_mats, dual, dual_r, short, rhs)
    rows, x, xr = call(
        project_kernel, [((waves, columns), F32), field, rounded]
    )(solve(payload, False), w_hi, w_lo, res)
    rho = direction = None
    for step in range(ITERS):
        pre, payload = apply("mid", d_mats, x, xr, tall)
        old = () if step == 0 else (rho, direction)
        rho, direction, dir_r = call(
            functools.partial(search_kernel, step == 0), [((8, columns), F32), field, rounded]
        )(solve(payload, True), w_hi, w_lo, pre, *old)
        if step < ITERS - 1:
            image, payload = apply("mid", n_mats, direction, dir_r, tall)
            dual, res, x, xr = call(step_kernel, [field, field, field, rounded])(
                solve(payload, True), w_hi, w_lo, rho, direction, image, dual, res, rows
            )
        else:
            image, payload = apply("last", n_mats, direction, dir_r, 8)
            got = exchange(payload, GATHER)
            terms, = call(partial_kernel, [((groups * near, 8, half), F32)])(got)
            dual, res = call(final_kernel, [field, field])(
                exchange(terms, SPREAD), rho, direction, image, dual, res
            )
    return dual[None, None], res[None, None]


def solution(mesh):
    finer = Mesh(mesh.devices.reshape(mesh.shape["grp"], 8, 4, 2), ("grp", "z", "x", "c"))
    spec = P("grp", SUB, None, None)

    return jax.shard_map(
        shards,
        mesh=finer,
        in_specs=(spec, spec, spec, spec, P("grp", SUB), P("grp", SUB, None)),
        out_specs=(spec, spec),
        check_vma=False,
    )
```

```python
import functools

import jax
import jax.numpy as jnp
from jax import lax
from jax.experimental import pallas as pl
from jax.experimental.pallas import tpu as pltpu
from jax.sharding import Mesh
from jax.sharding import PartitionSpec as P

NDIR = 64
ITERS = 2
WAVE_NUMBER = 0.785
SUB = ("z", "x", "c")
GATHER = ("z", "c")
SPREAD = ("grp", "x")
F32 = jnp.float32
BF16 = jnp.bfloat16
GRANT = pltpu.CompilerParams(vmem_limit_bytes=14 << 20)


def call(body, outs, flops=0, size=0):
    return pl.pallas_call(
        body,
        out_shape=[jax.ShapeDtypeStruct(shape, dtype) for shape, dtype in outs],
        compiler_params=GRANT,
        cost_estimate=pl.CostEstimate(flops=flops, bytes_accessed=size, transcendentals=0),
    )


def mm(a, b):
    return jnp.dot(a, b, preferred_element_type=F32)


def halves(value):
    high = value.astype(BF16)
    return high, (value - high.astype(F32)).astype(BF16)


def mm_wide(pair, value):
    high, low = halves(value)
    return mm(pair[0], high) + (mm(pair[0], low) + mm(pair[1], high))


def reversal(n):
    rows = lax.broadcasted_iota(jnp.int32, (n, n), 0)
    cols = lax.broadcasted_iota(jnp.int32, (n, n), 1)
    return (rows + cols == n - 1).astype(BF16)


def live_rows(size_ref, shape):
    return lax.broadcasted_iota(jnp.int32, shape, 0) < size_ref[0, 0]


def wave_parts(size, directions, reach):
    def basis(axis):
        def along(v):
            return v[:, None] if axis == 0 else v[None, :]

        def across(v):
            return v[None, :] if axis == 0 else v[:, None]

        rows = jnp.arange(reach).astype(F32)
        live = (jnp.arange(reach) < size).astype(F32)
        angle = 2.0 * jnp.pi * directions.astype(F32) / NDIR
        phase = (jnp.arange(directions.shape[0]) % 2).astype(F32) * (jnp.pi / 2.0)
        wave = jnp.cos(WAVE_NUMBER * along(rows) * across(jnp.cos(angle)) + across(phase))
        wave = wave * along(live) / jnp.sqrt(F32(reach))
        high = lax.reduce_precision(wave, 8, 7)
        return high.astype(BF16), (wave - high).astype(BF16)

    return basis(0), basis(1)


STEPS = 14


def exponent(value):
    return jnp.ceil(jnp.log2(jnp.maximum(value, 1e-30)))


def scale_of(power):
    return jnp.exp2(STEPS - power)


def side_by_side(rows):
    half = rows.shape[1] // 2
    return [rows[:, :half], rows[:, half:]]


def coded_sum(extra):
    power = exponent(jnp.abs(extra))
    value = extra * scale_of(power)
    first = jnp.round(value)
    rest = jnp.round((value - first) * 2.0**STEPS)
    return side_by_side(power) + side_by_side(first) + side_by_side(rest)


def pack(blocks, code, out_ref, copies):
    count, waves, columns = blocks.shape
    half = columns // 2
    power = exponent(jnp.max(jnp.abs(blocks), axis=1))
    scaled = jnp.round(blocks * scale_of(power)[:, None, :]).astype(jnp.int32).astype(jnp.int16)
    for k in range(count):
        tail = side_by_side(power[k : k + 1]) + code
        tail = jnp.concatenate(tail, axis=0).astype(jnp.int32).astype(jnp.int16)
        for i in copies[k]:
            out_ref[i, 0:waves] = scaled[k, :, :half]
            out_ref[i, waves : 2 * waves] = scaled[k, :, half:]
            out_ref[i, 2 * waves :] = tail


def no_sum(columns):
    return [jnp.zeros((1, columns // 2), F32)] * 6


def wide(value):
    return value.astype(jnp.int32).astype(F32)


def unpack(value, waves, extra):
    tail = wide(value[2 * waves :])
    back = 1.0 / scale_of(tail[0:4])
    rows = jnp.concatenate(
        [wide(value[0:waves]) * back[0:1], wide(value[waves : 2 * waves]) * back[1:2]], axis=1
    )
    if not extra:
        return rows, None
    sums = (tail[4:6] + tail[6:8] * 2.0**-STEPS) * back[2:4]
    return rows, jnp.concatenate([sums[0:1], sums[1:2]], axis=1)


def coded(value, out_ref):
    rows, columns = value.shape
    power = exponent(jnp.max(jnp.abs(value), axis=0, keepdims=True))
    out_ref[0:rows] = jnp.round(value * scale_of(power)).astype(jnp.int32).astype(jnp.int16)
    power = jnp.broadcast_to(power, (16, columns))
    out_ref[rows:] = power.astype(jnp.int32).astype(jnp.int16)


def decoded(ref):
    value = ref[...]
    rows = value.shape[0] - 16
    return wide(value[0:rows]) * (1.0 / scale_of(wide(value[rows:])[0:1]))


def heads_kernel(mat_ref, loads_ref, out_ref):
    reach = out_ref.shape[0] - 16
    coded(mm(mat_ref[0:reach], loads_ref[...]), out_ref)


def turn_kernel(mat_ref, own_ref, away_ref):
    reach = own_ref.shape[0]
    flip = reversal(reach)
    low = mm(flip, mat_ref[reach:]).astype(BF16)
    own_ref[:, 0:reach] = mm(low[:, reach:], flip).astype(BF16)
    own_ref[:, reach:] = low[:, :reach]
    away_ref[:, 0:reach] = mat_ref[0:reach, 0:reach]
    away_ref[:, reach:] = mm(mat_ref[0:reach, reach:], flip).astype(BF16)


def tile_kernel(near, far, place_ref, tile_ref, out_ref, *rest):
    *away_refs, all_ref = rest
    place = place_ref[0, 0]
    waves = tile_ref.shape[1] // (near * far)
    value = tile_ref[...]
    for j in range(near):
        pieces = [value[:, (k * near + j) * waves : (k * near + j + 1) * waves] for k in range(far)]
        coded(jnp.concatenate(pieces, axis=1), all_ref.at[lax.rem(j + near - place, near)])
    for d, ref in enumerate((out_ref, *away_refs)):
        ref[...] = all_ref[d]


def parts_kernel(place_ref, *refs):
    *got_refs, out_ref = refs
    near = len(got_refs)
    rows = out_ref.shape[1] // 2
    for d, ref in enumerate(got_refs):
        source = lax.rem(place_ref[0, 0] + near - d, near)
        high, low = halves(decoded(ref))
        out_ref[source, 0:rows] = high
        out_ref[source, rows:] = low


def rhs_kernel(size_ref, mat_ref, loads_ref, heads_ref, wt_hi, wt_lo, rhs_ref, pay_ref):
    reach = rhs_ref.shape[0]
    turned = mm(reversal(reach), loads_ref[reach:]).astype(BF16)
    tails = mm(mat_ref[:, reach:], loads_ref[0:reach]) + mm(mat_ref[:, 0:reach], turned)
    rhs = jnp.where(live_rows(size_ref, tails.shape), tails - decoded(heads_ref), 0.0)
    rhs_ref[...] = rhs
    rows = mm_wide((wt_hi[...], wt_lo[...]), rhs)
    pack(rows[None], no_sum(rows.shape[1]), pay_ref, [range(pay_ref.shape[0])])


def inner_kernel(own_ref, away_ref, xr_ref, out_ref):
    reach = out_ref.shape[0]
    xr = xr_ref[...]
    out_ref[...] = mm(own_ref[:, 0:reach], xr) + mm(away_ref[:, 0:reach], xr)


def apply_kernel(mode, size_ref, own_ref, away_ref, inner_ref, x_ref, prev_ref, next_ref, wt_hi, wt_lo, *rest):
    reach = inner_ref.shape[0]
    outer = mm(own_ref[:, reach:], prev_ref[...]) + mm(away_ref[:, reach:], next_ref[...])
    product = inner_ref[...] - outer
    product = jnp.where(live_rows(size_ref, product.shape), product, 0.0)
    if mode == "start":
        rhs_ref, out_ref, pay_ref = rest
        product = rhs_ref[...] - product
        extra = None
    else:
        out_ref, pay_ref = rest
        extra = jnp.sum(x_ref[...] * product, axis=0, keepdims=True)
    out_ref[...] = product
    if mode == "last":
        half = extra.shape[1] // 2
        for i in range(pay_ref.shape[0]):
            pay_ref[i, 0:1] = extra[:, :half]
            pay_ref[i, 1:2] = extra[:, half:]
        return
    rows = mm_wide((wt_hi[...], wt_lo[...]), product)
    code = no_sum(rows.shape[1]) if extra is None else coded_sum(extra)
    pack(rows[None], code, pay_ref, [range(pay_ref.shape[0])])


def coarse_kernel(extra, groups, tiles_ref, got_ref, out_ref):
    near, twice, _ = tiles_ref.shape
    height = twice // 2
    waves = height // groups
    far = got_ref.shape[0]
    parts = [unpack(got_ref[k], waves, extra) for k in range(far)]
    stacked = jnp.concatenate([p[0] for p in parts], axis=0)
    if extra:
        code = coded_sum(sum([p[1] for p in parts[1:]], parts[0][1]))
    else:
        code = no_sum(stacked.shape[1])
    high, low = halves(stacked)
    for j in range(near):
        top = tiles_ref[j, 0:height]
        value = mm(top, high) + (mm(top, low) + mm(tiles_ref[j, height:], high))
        blocks = value.reshape(groups, waves, value.shape[1])
        pack(blocks, code, out_ref, [(h * near + j,) for h in range(groups)])


def summed(ref):
    total = ref[0]
    for i in range(1, ref.shape[0]):
        total = total + ref[i]
    return total


def gathered(ref, waves, extra):
    rows, row = unpack(ref[0], waves, extra)
    for i in range(1, ref.shape[0]):
        more, more_row = unpack(ref[i], waves, extra)
        rows = rows + more
        row = row + more_row if extra else None
    return rows, row


def lift(w_hi, w_lo, rows):
    return mm_wide((w_hi[...], w_lo[...]), rows)


def first_kernel(got_ref, w_hi, w_lo, dual_ref, dualr_ref):
    rows, _ = gathered(got_ref, w_hi.shape[1], False)
    dual = lift(w_hi, w_lo, rows)
    dual_ref[...] = dual
    dualr_ref[...] = dual.astype(BF16)


def project_kernel(got_ref, w_hi, w_lo, res_ref, rows_ref, out_ref, outr_ref):
    rows, _ = gathered(got_ref, w_hi.shape[1], False)
    rows_ref[...] = rows
    out = res_ref[...] - lift(w_hi, w_lo, rows)
    out_ref[...] = out
    outr_ref[...] = out.astype(BF16)


def search_kernel(first, got_ref, w_hi, w_lo, pre_ref, *rest):
    rows, rho = gathered(got_ref, w_hi.shape[1], True)
    out = pre_ref[...] - lift(w_hi, w_lo, rows)
    if first:
        rho_ref, out_ref, outr_ref = rest
    else:
        old_rho, old_dir, rho_ref, out_ref, outr_ref = rest
        out = out + rho / old_rho[0:1] * old_dir[...]
    rho_ref[...] = jnp.broadcast_to(rho, rho_ref.shape)
    out_ref[...] = out
    outr_ref[...] = out.astype(BF16)


def step_kernel(got_ref, w_hi, w_lo, rho_ref, dir_ref, img_ref, dual_ref, res_ref, rows_ref,
                new_dual, new_res, new_out, new_outr):
    rows, bottom = gathered(got_ref, w_hi.shape[1], True)
    alpha = rho_ref[0:1] / bottom
    new_dual[...] = dual_ref[...] + alpha * dir_ref[...]
    res = res_ref[...] - alpha * img_ref[...]
    new_res[...] = res
    out = res - lift(w_hi, w_lo, rows_ref[...] - alpha * rows)
    new_out[...] = out
    new_outr[...] = out.astype(BF16)


def partial_kernel(got_ref, out_ref):
    total = summed(got_ref)
    for i in range(out_ref.shape[0]):
        out_ref[i] = total


def final_kernel(got_ref, rho_ref, dir_ref, img_ref, dual_ref, res_ref, new_dual, new_res):
    total = summed(got_ref)
    bottom = jnp.concatenate([total[0:1], total[1:2]], axis=1)
    alpha = rho_ref[0:1] / bottom
    new_dual[...] = dual_ref[...] + alpha * dir_ref[...]
    new_res[...] = res_ref[...] - alpha * img_ref[...]


def passed_along(block, distance):
    n = lax.axis_size(SUB)
    return lax.ppermute(block, SUB, [((i - distance) % n, i) for i in range(n)])


def exchange(value, axes):
    return lax.all_to_all(value, axes, 0, 0, tiled=True)


def shards(neumann, dirichlet, coarse_inverse, loads, iface_sizes, wave_dirs):
    nmat, dmat = neumann[0, 0], dirichlet[0, 0]
    tile, load = coarse_inverse[0, 0], loads[0, 0]
    width, columns = load.shape
    reach = width // 2
    directions = wave_dirs[0, 0]
    waves = directions.shape[0]
    groups = lax.axis_size("grp")
    near = lax.axis_size("x")
    far = lax.axis_size(GATHER)
    half = columns // 2
    size = iface_sizes
    field, rounded = ((reach, columns), F32), ((reach, columns), BF16)

    heads, = call(heads_kernel, [((reach + 16, columns), jnp.int16)], 2 * reach * width * columns, 2 << 20)(nmat, load)
    heads = passed_along(heads, -1)
    place = lax.axis_index("x").astype(jnp.int32).reshape(1, 1)
    smem = pl.BlockSpec(memory_space=pltpu.SMEM)
    vmem = pl.BlockSpec(memory_space=pltpu.VMEM)
    block = ((tile.shape[0] + 16, tile.shape[1] // near), jnp.int16)
    kept, *sent = pl.pallas_call(
        functools.partial(tile_kernel, near, lax.axis_size("z")),
        out_shape=[jax.ShapeDtypeStruct(*block)] * near,
        in_specs=[smem, vmem],
        scratch_shapes=[pltpu.VMEM((near, *block[0]), block[1])],
        name="tile",
        compiler_params=GRANT,
    )(place, tile)
    came = [
        lax.ppermute(sent[d - 1], "x", [(i, (i + d) % near) for i in range(near)])
        for d in range(1, near)
    ]
    tiles = pl.pallas_call(
        parts_kernel,
        out_shape=jax.ShapeDtypeStruct((near, 2 * tile.shape[0], tile.shape[1] // near), BF16),
        in_specs=[smem] + [vmem] * near,
        name="parts",
        compiler_params=GRANT,
    )(place, kept, *came)
    turn = call(turn_kernel, [((reach, width), BF16)] * 2, 6 * reach**3, 4 << 20)
    n_own, n_away = turn(nmat)
    n_away = passed_along(n_away, -1)
    d_own, d_away = turn(dmat)
    d_away = pltpu.with_memory_space_constraint(passed_along(d_away, -1), pltpu.VMEM)

    (w_hi, w_lo), (wt_hi, wt_lo) = wave_parts(size[0, 0], directions, reach)

    short = tall = 2 * waves + 8
    flops = 2 * reach * 2 * width * columns

    def pay(rows):
        return ((far, rows, half), F32 if rows == 8 else jnp.int16)

    def solve(payload, extra):
        got = exchange(payload, GATHER)
        terms, = call(
            functools.partial(coarse_kernel, extra, groups),
            [((groups * near, got.shape[1], half), jnp.int16)],
            6 * near * 4 * waves * far * waves * columns,
            2 << 20,
        )(tiles, got)
        return exchange(terms, SPREAD)

    def halo(rounded_x):
        return passed_along(rounded_x, 1), passed_along(rounded_x, -1)

    def apply(mode, mats, x, xr, rows, *rest):
        before, after = halo(xr)
        inner, = call(inner_kernel, [field], flops // 2, 1 << 20)(*mats, xr)
        smem = pl.BlockSpec(memory_space=pltpu.SMEM)
        vmem = pl.BlockSpec(memory_space=pltpu.VMEM)
        count = 8 + len(rest)
        return pl.pallas_call(
            functools.partial(apply_kernel, mode),
            out_shape=[
                jax.ShapeDtypeStruct(*field),
                jax.ShapeDtypeStruct(*pay(rows)),
            ],
            in_specs=[smem] + [vmem] * count,
            compiler_params=GRANT,
            cost_estimate=pl.CostEstimate(flops=flops, bytes_accessed=4 << 20, transcendentals=0),
        )(size, mats[0], mats[1], inner, x, before, after, wt_hi, wt_lo, *rest)

    rhs, payload = pl.pallas_call(
        rhs_kernel,
        out_shape=[jax.ShapeDtypeStruct(*field), jax.ShapeDtypeStruct(*pay(short))],
        in_specs=[pl.BlockSpec(memory_space=pltpu.SMEM)]
        + [pl.BlockSpec(memory_space=pltpu.VMEM)] * 5,
        name="rhs",
        compiler_params=GRANT,
    )(size, n_own, load, heads, wt_hi, wt_lo)

    n_mats, d_mats = (n_own, n_away), (d_own, d_away)
    dual, dual_r = call(first_kernel, [field, rounded])(solve(payload, False), w_hi, w_lo)
    res, payload = apply("start", n_mats, dual, dual_r, short, rhs)
    rows, x, xr = call(
        project_kernel, [((waves, columns), F32), field, rounded]
    )(solve(payload, False), w_hi, w_lo, res)
    rho = direction = None
    for step in range(ITERS):
        pre, payload = apply("mid", d_mats, x, xr, tall)
        old = () if step == 0 else (rho, direction)
        rho, direction, dir_r = call(
            functools.partial(search_kernel, step == 0), [((8, columns), F32), field, rounded]
        )(solve(payload, True), w_hi, w_lo, pre, *old)
        if step < ITERS - 1:
            image, payload = apply("mid", n_mats, direction, dir_r, tall)
            dual, res, x, xr = call(step_kernel, [field, field, field, rounded])(
                solve(payload, True), w_hi, w_lo, rho, direction, image, dual, res, rows
            )
        else:
            image, payload = apply("last", n_mats, direction, dir_r, 8)
            got = exchange(payload, GATHER)
            terms, = call(partial_kernel, [((groups * near, 8, half), F32)])(got)
            dual, res = call(final_kernel, [field, field])(
                exchange(terms, SPREAD), rho, direction, image, dual, res
            )
    return dual[None, None], res[None, None]


def solution(mesh):
    finer = Mesh(mesh.devices.reshape(mesh.shape["grp"], 8, 4, 2), ("grp", "z", "x", "c"))
    spec = P("grp", SUB, None, None)

    return jax.shard_map(
        shards,
        mesh=finer,
        in_specs=(spec, spec, spec, spec, P("grp", SUB), P("grp", SUB, None)),
        out_specs=(spec, spec),
        check_vma=False,
    )
```
